32 devices in a mesh: leaf: 4 (over z), agg: 2 (over core), probe: 4 (over y, x).
Axes of the slice: x: 2, y: 2, z: 4, core: 2. Of those that a mesh axis runs over, the one named last changes fastest.
Arguments:
- probes: float32 [4, 192, 1024], P('probe', None, ('leaf', 'agg')), may hold values from -16 to 16
- viscosity: float32 [192, 1024], P(None, ('leaf', 'agg')), may hold values from 0.1 to 10
- friction: float32 [192, 1024], P(None, ('leaf', 'agg')), may hold values from 0.05 to 1
- sensitivity: float32 [192, 1024], P(None, ('leaf', 'agg')), may hold values from 0.5 to 3
- misfit_weight: float32 [192, 1024], P(None, ('leaf', 'agg')), may hold values from 1 to 10
- grad_ref: float32 [192, 192], replicated, may hold values from -2 to 3, as said below
- trace_ref: float32 [192, 192], replicated, may hold values from -2 to 3
- coarse_modes: float32 [192, 128], replicated, may hold values from -0.4375 to 0.4375
- coarse_inv: float32 [64, 128, 128], P(('leaf', 'agg')), may hold values from -1 to 5, as said below
- peer_slots: int32 [8, 8, 16], P(('leaf', 'agg')), may hold values from -1 to 127, as said below
- local_pairs: int32 [2, 1024], P(None, ('leaf', 'agg')), may hold values from 0 to 127, as said below
- elem_agg: int32 [1024], P(('leaf', 'agg')), may hold values from 0 to 15
Outputs:
- incr_velocity: float32 [4, 192, 1024], P('probe', None, ('leaf', 'agg'))
- hess_action: float32 [4, 192, 1024], P('probe', None, ('leaf', 'agg'))
- trace_est: float32 [], replicated
The draws below stay inside these ranges and needn't reach their ends.
Inputs may be any that keep to these rules, and one draw needn't show every extreme that they name: `grad_ref`: nonsingular. `coarse_inv`: each block is symmetric positive definite. peer_slots[P, Q, s] >= 0 exactly when peer_slots[Q, P, s] >= 0; the filled slots of a pair come first; no slot of a pair P, P is filled; the partitions are blocks of a three-dimensional grid and only blocks that touch by a face, edge or corner share slots, so a partition has at most 26 partners; some pair of partitions fills all 16 slots. `local_pairs`: the two elements of a pair differ.
All inputs are finite; a program needn't handle non-finite values.
Results may differ from the reference program's by a relative error of at most 0.0003.
Values sent between devices are 32-bit elements; how exact they have to be, the bound alone decides.
No kernel may reach another device: no remote copies, remote signals or barrier semaphores. Data moves between devices by JAX's collectives and lax.ppermute only.
A program may use at most 64 MiB of HBM per device.

```python
import math
import jax
import jax.numpy as jnp
from jax import lax

NDOF = 192
CW = 128
E_DEV = 128
AGG_DEV = 8
CAP = 16
ITERS = 2
SWEEPS = 3
NPART = 8
NE = 1024
NAGG = 64
GROUP_AGG = 16
NLP = 1024
PROBES = 4
N_LEAF = 4
N_AGG = 2


def draw_probes(key, part):
    subkey = jax.random.fold_in(key, 11)
    fraction = jnp.arange(NE, dtype=jnp.float32) / NE
    base = jnp.clip(jax.random.normal(subkey, (PROBES, NDOF, NE), jnp.float32), -4.0, 4.0)
    profile = jnp.exp(math.log(3.0) * fraction)
    return base * profile[None, None, :]


def near_identity(noise, factor):
    return factor * (jnp.eye(NDOF, dtype=jnp.float32) + 0.4 * noise / math.sqrt(NDOF))


def draw_grad_ref(key, part):
    subkey = jax.random.fold_in(key, 21)
    noise = jnp.clip(jax.random.normal(subkey, (NDOF, NDOF), jnp.float32), -4.0, 4.0)
    return near_identity(noise, 1.0)


def draw_trace_ref(key, part):
    subkey = jax.random.fold_in(key, 22)
    noise = jnp.clip(jax.random.normal(subkey, (NDOF, NDOF), jnp.float32), -4.0, 4.0)
    return near_identity(noise, 0.5)


def draw_coarse_inv(key, part):
    first_key = jax.random.fold_in(key, 31)
    second_key = jax.random.fold_in(key, 32)
    bound_off = 2.0 / CW
    upper = jax.random.uniform(first_key, (NAGG, CW, CW), jnp.float32, -bound_off, bound_off)
    symmetric = 0.5 * (upper + jnp.transpose(upper, (0, 2, 1)))
    diagonal = jnp.exp(jax.random.uniform(second_key, (NAGG, CW), jnp.float32, math.log(2.5), math.log(5.0)))
    identity = jnp.eye(CW, dtype=jnp.float32)
    factor = 1.0 / math.sqrt(max(E_DEV // AGG_DEV, 1))
    return factor * (symmetric * (1.0 - identity)[None] + identity[None] * diagonal[:, :, None])


def grid_place(index_part):
    half_rest = NPART // 8
    coord_x = index_part % 4
    rest = index_part // 4
    folded = 2 * (rest % half_rest) + rest // half_rest
    return (coord_x, folded % 4, folded // 4)


def draw_peer_slots(key, part):
    weight_key = jax.random.fold_in(key, 41)
    count_key = jax.random.fold_in(key, 42)
    first_key = jax.random.fold_in(key, 43)
    second_key = jax.random.fold_in(key, 44)
    elem_key = jax.random.fold_in(key, 45)
    index_part = jnp.arange(NPART, dtype=jnp.int32)
    coord_x, coord_y, coord_z = grid_place(index_part)
    touching = (jnp.abs(coord_x[:, None] - coord_x[None, :]) <= 1) & (jnp.abs(coord_y[:, None] - coord_y[None, :]) <= 1) & (jnp.abs(coord_z[:, None] - coord_z[None, :]) <= 1)
    weights = jax.random.randint(weight_key, (NPART,), 1, 5)
    raw_counts = jax.random.randint(count_key, (NPART, NPART), CAP // 2, CAP + 1)
    rows = index_part[:, None]
    cols = index_part[None, :]
    paired = jnp.where(rows < cols, raw_counts, raw_counts.T)
    counts = jnp.minimum(CAP, jnp.maximum(1, paired * (weights[:, None] + weights[None, :]) // 5))
    counts = jnp.where(touching & (rows != cols), counts, 0)
    first_part = 4 * jax.random.randint(first_key, (), 0, NPART // 4) + jax.random.randint(second_key, (), 0, 3)
    second_part = first_part + 1
    full_pair = (rows == first_part) & (cols == second_part) | (rows == second_part) & (cols == first_part)
    counts = jnp.where(full_pair, CAP, counts)
    elements = jax.random.randint(elem_key, (NPART, NPART, CAP), 0, E_DEV)
    slot_index = jnp.arange(CAP)[None, None, :]
    return jnp.where(slot_index < counts[:, :, None], elements, -1).astype(jnp.int32)


def draw_local_pairs(key, part):
    first_key = jax.random.fold_in(key, 51)
    second_key = jax.random.fold_in(key, 52)
    first_end = jax.random.randint(first_key, (NLP,), 0, E_DEV)
    offset = jax.random.randint(second_key, (NLP,), 1, E_DEV)
    second_end = (first_end + offset) % E_DEV
    return jnp.stack([first_end, second_end]).astype(jnp.int32)


def touch_ends(values, rng, smallest, top_value):
    longest = values.shape.index(max(values.shape))
    spots = []
    for shift in (0, 1):
        where = [jax.random.randint(jax.random.fold_in(rng, axis), (), 0, length) for axis, length in enumerate(values.shape)]
        where[longest] = (where[longest] + shift) % values.shape[longest]
        spots.append(tuple(where))
    return values.at[spots[0]].set(smallest).at[spots[1]].set(top_value)


def block_scale(stream_key, extent, cuts, low, high):
    def one(dim, shards_of):
        steps = jax.random.uniform(jax.random.fold_in(jax.random.fold_in(stream_key, 6), dim), (shards_of,), jnp.float32, low / len(cuts), high / len(cuts))
        return jnp.repeat(jnp.exp(steps), extent[dim] // shards_of).reshape((-1,) + (1,) * (len(extent) - dim - 1))

    gain = one(*cuts[0])
    for cut in cuts[1:]:
        gain = gain * one(*cut)
    return gain


def normal_values(key, shape, deviation, bound, kind=jnp.bfloat16):
    return jnp.clip(deviation * jax.random.normal(key, shape, jnp.float32), -bound, bound).astype(kind)


def setup_inputs(seed: int = 0) -> dict:
    streams_of = jax.random.split(jax.random.key(seed), 13)
    return {
        "probes": draw_probes(jax.random.fold_in(streams_of[12], 71), 0),
        "viscosity": jnp.clip(jnp.exp(math.log(10.0) - 4.6051702 * jax.random.uniform(streams_of[1], (NDOF, NE), jnp.float32) ** block_scale(streams_of[1], (NDOF, NE), ((1, 8),), -0.2, 0.2)), 0.1, 10.0),
        "friction": jnp.clip(jnp.exp(math.log(1.0) - 2.9957323 * jax.random.uniform(streams_of[2], (NDOF, NE), jnp.float32) ** block_scale(streams_of[2], (NDOF, NE), ((1, 8),), -0.2, 0.2)), 0.05, 1.0),
        "sensitivity": jnp.clip(jnp.exp(math.log(3.0) - 1.7917595 * jax.random.uniform(streams_of[3], (NDOF, NE), jnp.float32) ** block_scale(streams_of[3], (NDOF, NE), ((1, 8),), -0.2, 0.2)), 0.5, 3.0),
        "misfit_weight": jnp.clip(jnp.exp(math.log(10.0) - 2.3025851 * jax.random.uniform(streams_of[4], (NDOF, NE), jnp.float32) ** block_scale(streams_of[4], (NDOF, NE), ((1, 8),), -0.2, 0.2)), 1.0, 10.0),
        "grad_ref": draw_grad_ref(jax.random.fold_in(streams_of[12], 71), 0),
        "trace_ref": draw_trace_ref(jax.random.fold_in(streams_of[12], 71), 0),
        "coarse_modes": normal_values(streams_of[7], (NDOF, CW), NDOF ** -0.5, 0.4375, jnp.float32),
        "coarse_inv": draw_coarse_inv(jax.random.fold_in(streams_of[12], 71), 0),
        "peer_slots": draw_peer_slots(jax.random.fold_in(streams_of[12], 71), 0),
        "local_pairs": draw_local_pairs(jax.random.fold_in(streams_of[12], 71), 0),
        "elem_agg": touch_ends(jax.random.randint(streams_of[11], (NE,), 0, GROUP_AGG), jax.random.fold_in(streams_of[11], 1), 0, GROUP_AGG - 1).astype(jnp.int32),
    }


highest = lax.Precision.HIGHEST
relax_weight = 0.6


def matmul(left, right):
    return jnp.dot(left, right, precision=highest, preferred_element_type=jnp.float32)


def reference(probes, viscosity, friction, sensitivity, misfit_weight, grad_ref, trace_ref, coarse_modes, coarse_inv, peer_slots, local_pairs, elem_agg):
    part_total = N_LEAF * N_AGG
    elem_total = E_DEV * part_total
    part_index = jnp.arange(part_total, dtype=jnp.int32)
    filled = peer_slots >= 0
    mirror = jnp.transpose(peer_slots, (1, 0, 2))
    own_global = jnp.where(filled, part_index[:, None, None] * E_DEV + peer_slots, 0).reshape(-1).astype(jnp.int32)
    other_global = jnp.where(filled, part_index[None, :, None] * E_DEV + mirror, 0).reshape(-1).astype(jnp.int32)
    filled_float = filled.reshape(-1).astype(jnp.float32)
    pair_base = ((jnp.arange(local_pairs.shape[1], dtype=jnp.int32) // E_DEV) * E_DEV).astype(jnp.int32)
    first_end = (local_pairs[0] + pair_base).astype(jnp.int32)
    second_end = (local_pairs[1] + pair_base).astype(jnp.int32)
    counts = jnp.zeros((elem_total,), jnp.float32)
    counts = counts.at[first_end].add(1.0).at[second_end].add(1.0).at[own_global].add(filled_float)
    trace_square = jnp.sum(trace_ref * trace_ref, axis=0)
    diag_op = matmul((grad_ref * grad_ref).T, viscosity) + friction + counts[None, :] * trace_square[:, None]
    agg_index = ((jnp.arange(elem_total, dtype=jnp.int32) // (E_DEV * N_AGG)) * GROUP_AGG + elem_agg).astype(jnp.int32)

    def operate(field_vec):
        inner_term = matmul(grad_ref.T, viscosity * matmul(grad_ref, field_vec))
        traces = matmul(trace_ref, field_vec)
        local_diff = traces[:, first_end] - traces[:, second_end]
        cross_diff = (traces[:, own_global] - traces[:, other_global]) * filled_float[None, :]
        accumulated = jnp.zeros_like(field_vec)
        accumulated = accumulated.at[:, first_end].add(local_diff).at[:, second_end].add(-local_diff)
        accumulated = accumulated.at[:, own_global].add(cross_diff)
        return inner_term + friction * field_vec + matmul(trace_ref.T, accumulated)

    def coarse(residual_now):
        projected = matmul(coarse_modes.T, residual_now)
        coarse_sums = jax.ops.segment_sum(projected.T, agg_index, num_segments=NAGG).T
        solved = jnp.einsum("acd,da->ca", coarse_inv, coarse_sums, precision=highest)
        return matmul(coarse_modes, solved[:, agg_index])

    def precond(residual_now):
        smooth = relax_weight * residual_now / diag_op
        for sweep_index in range(SWEEPS - 1):
            smooth = smooth + relax_weight * (residual_now - operate(smooth)) / diag_op
        return smooth + coarse(residual_now)

    def krylov(source):
        residual_now = source
        precon = precond(residual_now)
        search = precon
        energy_now = jnp.sum(residual_now * precon)
        iterate = jnp.zeros_like(source)
        for iteration in range(ITERS):
            image_vec = operate(search)
            step_size = energy_now / jnp.sum(search * image_vec)
            iterate = iterate + step_size * search
            if iteration + 1 < ITERS:
                residual_now = residual_now - step_size * image_vec
                precon = precond(residual_now)
                energy_next = jnp.sum(residual_now * precon)
                search = precon + (energy_next / energy_now) * search
                energy_now = energy_next
        return iterate

    velocities = []
    hessians = []
    for probe_index in range(PROBES):
        forward = krylov(sensitivity * probes[probe_index])
        adjoint = krylov(misfit_weight * forward)
        velocities.append(forward)
        hessians.append(sensitivity * adjoint)
    velocity_stack = jnp.stack(velocities)
    hessian_stack = jnp.stack(hessians)
    trace_value = jnp.sum(probes * hessian_stack) / PROBES
    return velocity_stack, hessian_stack, trace_value
```

```python
import jax
import jax.numpy as jnp
from jax import lax
from jax.experimental import pallas as pl
from jax.experimental.pallas import tpu as pltpu
from jax.sharding import PartitionSpec as P

ITERS = 2
SWEEPS = 3


highest = lax.Precision.HIGHEST
relax_weight = 0.6
f32 = jnp.float32
bf16 = jnp.bfloat16


def matmul(left, right):
    return jnp.dot(left, right, precision=highest, preferred_element_type=jnp.float32)


def distributed(
    probes,
    viscosity,
    friction,
    sensitivity,
    misfit_weight,
    grad_ref,
    trace_ref,
    coarse_modes,
    coarse_inv,
    peer_slots,
    local_pairs,
    elem_agg,
):
    agg_count = lax.axis_size("agg")
    elem_local = viscosity.shape[1]
    slot_flat = peer_slots.reshape(-1)
    filled = slot_flat >= 0
    own_local = jnp.where(filled, slot_flat, 0)
    filled_float = filled.astype(jnp.float32)
    first_end = local_pairs[0]
    second_end = local_pairs[1]
    counts = jnp.zeros((elem_local,), jnp.float32)
    counts = counts.at[first_end].add(1.0).at[second_end].add(1.0).at[own_local].add(filled_float)
    trace_square = jnp.sum(trace_ref * trace_ref, axis=0)
    diag_op = (
        matmul((grad_ref * grad_ref).T, viscosity)
        + friction
        + counts[None, :] * trace_square[:, None]
    )
    group_aggs = agg_count * coarse_inv.shape[0]
    one_hot = (elem_agg[:, None] == jnp.arange(group_aggs, dtype=jnp.int32)[None, :]).astype(
        jnp.float32
    )

    def operate(field_vec):
        inner_term = matmul(grad_ref.T, viscosity * matmul(grad_ref, field_vec))
        traces = matmul(trace_ref, field_vec)
        outgoing = traces[:, own_local] * filled_float[None, :]
        incoming = lax.all_to_all(
            outgoing, ("leaf", "agg"), split_axis=1, concat_axis=1, tiled=True
        )
        cross_diff = outgoing - incoming
        local_diff = traces[:, first_end] - traces[:, second_end]
        accumulated = jnp.zeros_like(field_vec)
        accumulated = (
            accumulated.at[:, first_end].add(local_diff).at[:, second_end].add(-local_diff)
        )
        accumulated = accumulated.at[:, own_local].add(cross_diff)
        return inner_term + friction * field_vec + matmul(trace_ref.T, accumulated)

    def coarse(residual_now):
        projected = matmul(coarse_modes.T, residual_now)
        coarse_sums = matmul(projected, one_hot)
        own_sums = lax.psum_scatter(coarse_sums, "agg", scatter_dimension=1, tiled=True)
        solved_own = jnp.einsum("acd,da->ca", coarse_inv, own_sums, precision=highest)
        solved_all = lax.all_gather(solved_own, "agg", axis=1, tiled=True)
        return matmul(coarse_modes, matmul(solved_all, one_hot.T))

    def precond(residual_now):
        smooth = relax_weight * residual_now / diag_op
        for sweep_index in range(SWEEPS - 1):
            smooth = smooth + relax_weight * (residual_now - operate(smooth)) / diag_op
        return smooth + coarse(residual_now)

    def energy_sum(left, right):
        return lax.psum(jnp.sum(left * right), ("leaf", "agg"))

    def krylov(source):
        residual_now = source
        precon = precond(residual_now)
        search = precon
        energy_now = energy_sum(residual_now, precon)
        iterate = jnp.zeros_like(source)
        for iteration in range(ITERS):
            image_vec = operate(search)
            step_size = energy_now / lax.psum(jnp.sum(search * image_vec), ("leaf", "agg"))
            iterate = iterate + step_size * search
            if iteration + 1 < ITERS:
                residual_now = residual_now - step_size * image_vec
                precon = precond(residual_now)
                energy_next = energy_sum(residual_now, precon)
                search = precon + energy_next / energy_now * search
                energy_now = energy_next
        return iterate

    probe_field = probes[0]
    forward = krylov(sensitivity * probe_field)
    adjoint = krylov(misfit_weight * forward)
    action = sensitivity * adjoint
    trace_value = lax.psum(jnp.sum(probe_field * action), ("leaf", "agg", "probe")) / lax.axis_size(
        "probe"
    )
    return (forward[None], action[None], trace_value)


def split(value):
    high = value.astype(bf16)
    low = (value - high.astype(f32)).astype(bf16)
    return high, low


def dot(left, right):
    return jnp.dot(left, right, preferred_element_type=f32)


def dot_nt(left, right):
    return lax.dot_general(left, right, (((1,), (1,)), ((), ())), preferred_element_type=f32)


def total(value):
    return jnp.sum(jnp.sum(value, axis=0, keepdims=True), axis=1, keepdims=True)


def spec(space):
    return pl.BlockSpec(memory_space=space)


VM = pltpu.VMEM
SM = pltpu.SMEM


def call(kernel, name, outs, args, spaces=None, scratch=(), flops=0, bytes_accessed=0):
    spaces = spaces or [VM] * len(args)
    return pl.pallas_call(
        kernel,
        name=name,
        out_shape=[jax.ShapeDtypeStruct(*one) for one in outs],
        in_specs=[spec(space) for space in spaces],
        out_specs=[spec(VM) for _ in outs],
        scratch_shapes=list(scratch),
        compiler_params=pltpu.CompilerParams(vmem_limit_bytes=40 * 1024 * 1024),
        cost_estimate=pl.CostEstimate(
            flops=flops, bytes_accessed=bytes_accessed, transcendentals=0
        ),
    )(*args)


class Dims:
    def __init__(self, ndof, elem, parts, cap, modes, aggs):
        self.ndof, self.elem, self.parts, self.cap = ndof, elem, parts, cap
        self.modes, self.aggs = modes, aggs
        self.total = elem * parts
        self.half = parts // 2
        self.group = 2 * aggs
        self.all_aggs = parts * aggs
        self.chunk = 2 * elem


def prepare_kernel(dim, grad, grad_t, trace_t, modes, modes_t, g3, gs, gsq3, my, m3t, trsq):
    n = dim.ndof
    high, low = split(grad[...])
    g3[:, 0:n], g3[:, n : 2 * n], g3[:, 2 * n :] = high, high, low
    gt = grad_t[...]
    tt = trace_t[...]
    gram = lax.dot_general(
        tt, tt, (((1,), (1,)), ((), ())), precision=highest, preferred_element_type=f32
    )
    gh, gl = split(gt)
    sh, sl = split(gram)
    for place, piece in enumerate((gh, sh, gh, sh, gl, sl)):
        gs[:, place * n : (place + 1) * n] = piece
    qh, ql = split(gt * gt)
    gsq3[:, 0:n], gsq3[:, n : 2 * n], gsq3[:, 2 * n :] = qh, qh, ql
    mh, ml = split(modes[...])
    w = dim.modes
    my[:, 0:w], my[:, w : 2 * w], my[:, 2 * w :] = mh, mh, ml
    th, tl = split(modes_t[...])
    m3t[:, 0:n], m3t[:, n : 2 * n], m3t[:, 2 * n :] = th, th, tl
    trsq[...] = jnp.sum(tt * tt, axis=1, keepdims=True)


def prepare(dim, grad_ref, trace_ref, coarse_modes):
    n, w = dim.ndof, dim.modes
    return call(
        lambda *refs: prepare_kernel(dim, *refs),
        "prepare",
        [
            ((n, 3 * n), bf16),
            ((n, 6 * n), bf16),
            ((n, 3 * n), bf16),
            ((n, 3 * w), bf16),
            ((w, 3 * n), bf16),
            ((n, 1), f32),
        ],
        [grad_ref, grad_ref.T, trace_ref.T, coarse_modes, coarse_modes.T],
        flops=10**8,
        bytes_accessed=10**6,
    )


def restrict(dim, field, hot, m3t):
    high, low = split(field)
    sums = dot_nt(high, hot) + dot_nt(low, hot)
    high, low = split(sums)
    return dot(m3t[...], jnp.concatenate([high, low, high], axis=0))


def solve_blocks(sums, first, inv, count):
    rows = []
    for index in range(count):
        column = sums[:, first + index : first + index + 1]
        rows.append(jnp.sum(inv[index] * column, axis=0, keepdims=True))
    return jnp.concatenate(rows, axis=0)


def hot_of(dim, agg_row, agg_index, columns):
    place = lax.broadcasted_iota(jnp.int32, (dim.group, columns), 0)
    wanted = lax.rem(place + agg_index * dim.aggs, dim.group)
    return jnp.where(wanted.astype(f32) == agg_row, 1.0, 0.0).astype(bf16)


def source_kernel(dim, place, probe, sens, agg_row, m3t, source, sums):
    value = probe[...] * sens[...]
    source[...] = value
    hot = hot_of(dim, agg_row[...], 0, dim.elem)
    sums[...] = restrict(dim, value, hot, m3t)


def source_coarse_kernel(dim, place, sums_own, sums_partner, inv, out):
    sums = sums_own[...] + sums_partner[...]
    second = solve_blocks(sums, dim.aggs, inv, dim.aggs)
    first = solve_blocks(sums, 0, inv, dim.aggs)
    out[...] = jnp.where(place[1] == 0, first, second)


def block_of(dim, own, partner, rows, index):
    ref = own if index < dim.half else partner
    start = (index % dim.half) * rows
    return ref, start


def build_kernel(dim, place, own, partner, source, lap, hot2, counts, hot_own, table, sides, agg):
    n, e = dim.ndof, dim.elem
    rows = n + 8
    for index in range(dim.parts):
        ref, start = block_of(dim, own, partner, rows, index)
        where = place[4 + index]
        columns = pl.ds(pl.multiple_of(where * e, e), e)
        source[:, columns] = ref[start : start + n, :]
        sides[pl.ds(where, 1), :] = ref[start + n : start + n + 1, :]
        sides[pl.ds(where + dim.parts, 1), :] = ref[start + n + 1 : start + n + 2, :]
        table[pl.ds(where, 1), :] = ref[start + n + 2 : start + n + 3, :]
        group = (where // 2) * dim.group
        agg[:, columns] = ref[start + n + 3 : start + n + 4, :] + group.astype(f32)
    elem_id = lax.broadcasted_iota(jnp.int32, (e, e), 0).astype(f32)
    lane = lax.broadcasted_iota(jnp.int32, (e, e), 1)
    column_id = lax.broadcasted_iota(jnp.int32, (e, e), 1)
    row_id = lax.broadcasted_iota(jnp.int32, (e, e), 0)
    on_diagonal = row_id == column_id
    full = table[...]
    rolled = [full]
    for shift in range(1, dim.parts):
        rolled.append(pltpu.roll(full, shift * dim.cap, 1))
    slot_block = lane // dim.cap
    for p in range(dim.parts):
        mine = jnp.where(full[p : p + 1, :] == elem_id, 1.0, 0.0).astype(bf16)
        first = jnp.where(sides[p : p + 1, :] == elem_id, 1.0, 0.0)
        second = jnp.where(sides[p + dim.parts : p + dim.parts + 1, :] == elem_id, 1.0, 0.0)
        edge = (first - second).astype(bf16)
        local = dot_nt(edge, edge)
        count = jnp.sum(mine.astype(f32), axis=1, keepdims=True)
        for q in range(dim.parts):
            if q == p:
                block = local + jnp.where(on_diagonal, count, 0.0)
                diagonal = jnp.where(on_diagonal, block, 0.0)
                counts[:, p * e : (p + 1) * e] = jnp.sum(diagonal, axis=0, keepdims=True)
            else:
                row = rolled[(q - p) % dim.parts][q : q + 1, :]
                theirs = jnp.where((row == elem_id) & (slot_block == q), 1.0, 0.0).astype(bf16)
                block = -dot_nt(mine, theirs)
            lap[p * e : (p + 1) * e, q * e : (q + 1) * e] = block.astype(bf16)
    agg_id = lax.broadcasted_iota(jnp.int32, (dim.all_aggs, dim.total), 0).astype(f32)
    hot2[...] = jnp.where(agg[...] == agg_id, 1.0, 0.0).astype(bf16)
    leaf = place[0]
    span = 2 * e
    own_row = agg[:, pl.ds(pl.multiple_of(leaf * span, span), span)]
    own_row = own_row - (leaf * dim.group).astype(f32)
    hot_own[...] = hot_of(dim, own_row, place[1], span)


def chunks(dim):
    return [slice(start, start + dim.chunk) for start in range(0, dim.total, dim.chunk)]


def apply_operator(dim, vec, consts, v3, uy, emit):
    visc, fric, lap, g3, gs = consts
    n = dim.ndof
    for c in chunks(dim):
        high, low = split(vec[:, c])
        v3[0:n, c] = high
        v3[n : 2 * n, c] = low
        v3[2 * n : 3 * n, c] = high
    for c in chunks(dim):
        high, low = split(visc[:, c] * dot(g3[...], v3[:, c]))
        uy[0:n, c] = high
        uy[2 * n : 3 * n, c] = low
        uy[4 * n : 5 * n, c] = high
    for c in chunks(dim):
        both = dot(v3[0 : 2 * n, :], lap[:, c])
        high, low = split(both[0:n] + both[n : 2 * n])
        uy[n : 2 * n, c] = high
        uy[3 * n : 4 * n, c] = low
        uy[5 * n : 6 * n, c] = high
    for c in chunks(dim):
        emit(c, dot(gs[...], uy[:, c]) + fric[:, c] * vec[:, c])


def smooth_loop(dim, resid, smooth, w_diag, consts, v3, uy, nxt):
    for c in chunks(dim):
        smooth[:, c] = w_diag[:, c] * resid[:, c]

    def sweep(index, carry):
        def emit(c, image):
            smooth[:, c] = smooth[:, c] + w_diag[:, c] * (resid[:, c] - image)

        apply_operator(dim, smooth, consts, v3, uy, emit)
        return carry

    lax.fori_loop(0, SWEEPS - 1, sweep, 0)


def coarse_add(dim, solved, my, hot2, target):
    high, low = split(solved)
    coarse = dot_nt(my[...], jnp.concatenate([high, low, high], axis=1))
    high, low = split(coarse)
    for c in chunks(dim):
        target[:, c] = target[:, c] + dot(high, hot2[:, c]) + dot(low, hot2[:, c])


def group_solve(dim, place, resid, hot_own, m3t, inv_own, inv_partner, out):
    leaf, agg = place[0], place[1]
    span = 2 * dim.elem
    field = resid[:, pl.ds(pl.multiple_of(leaf * span, span), span)]
    sums = restrict(dim, field, hot_own[...], m3t)
    out[pl.ds(pl.multiple_of(agg * dim.aggs, dim.aggs), dim.aggs), :] = solve_blocks(
        sums, 0, inv_own, dim.aggs
    )
    out[pl.ds(pl.multiple_of((1 - agg) * dim.aggs, dim.aggs), dim.aggs), :] = solve_blocks(
        sums, dim.aggs, inv_partner, dim.aggs
    )


def first_step(dim, source, smooth, image, consts, v3, uy, resid, search, scal):
    n = dim.ndof

    def emit(c, value):
        image[:, c] = value

    apply_operator(dim, search, consts, v3, uy, emit)
    energy = total(source[...] * search[...])
    step = energy / total(search[...] * image[...])
    resid[...] = source[...] - step * image[...]
    scal[0:1, :] = jnp.broadcast_to(energy, (1, 128))
    scal[1:2, :] = jnp.broadcast_to(step, (1, 128))


def second_step(dim, resid, search, precon, scal, consts, v3, uy, image):
    energy = total(resid[...] * precon[...])
    ratio = energy / scal[0:1, 0:1]
    precon[...] = precon[...] + ratio * search[...]

    def emit(c, value):
        image[:, c] = value

    apply_operator(dim, precon, consts, v3, uy, emit)
    step = energy / total(precon[...] * image[...])
    precon[...] = scal[1:2, 0:1] * search[...] + step * precon[...]


def gather_parts(dim, place, parts, solved):
    for index, ref in enumerate(parts):
        where = place[4 + index] // 2
        solved[pl.ds(pl.multiple_of(where * dim.group, dim.group), dim.group), :] = ref[...]


def forward_kernel(
    dim, place, own, partner, source, counts, trsq, lap, g3, gs, gsq3, hot2, my, m3t, hot_own,
    inv_own, inv_partner,
    visc, fric, w_diag, search, resid, scal, out,
    v3, uy, image, solved,
):
    n, e = dim.ndof, dim.elem
    rows = 2 * n + dim.aggs
    for index in range(dim.parts):
        ref, start = block_of(dim, own, partner, rows, index)
        where = place[4 + index]
        columns = pl.ds(pl.multiple_of(where * e, e), e)
        visc[:, columns] = ref[start : start + n, :]
        fric[:, columns] = ref[start + n : start + 2 * n, :]
        solved[pl.ds(pl.multiple_of(where * dim.aggs, dim.aggs), dim.aggs), :] = ref[
            start + 2 * n : start + rows, :
        ]
    for c in chunks(dim):
        high, low = split(visc[:, c])
        diag = dot(gsq3[...], jnp.concatenate([high, low, high], axis=0))
        diag = diag + fric[:, c] + counts[:, c] * trsq[...]
        w_diag[:, c] = relax_weight / diag
    consts = (visc, fric, lap, g3, gs)
    smooth_loop(dim, source, search, w_diag, consts, v3, uy, image)
    coarse_add(dim, solved[...], my, hot2, search)
    first_step(dim, source, None, image, consts, v3, uy, resid, search, scal)
    group_solve(dim, place, resid, hot_own, m3t, inv_own, inv_partner, out)


def smooth_kernel(dim, resid, visc, fric, w_diag, lap, g3, gs, smooth, v3, uy):
    smooth_loop(dim, resid, smooth, w_diag, (visc, fric, lap, g3, gs), v3, uy, None)


def middle_kernel(
    dim, place, smooth, resid, search, scal, own, partner, visc, fric, lap, g3, gs, hot2, my, m3t,
    hot_own, inv_own, inv_partner, *refs,
):
    parts = refs[: dim.half]
    iterate, source, out, v3, uy, image, solved, precon = refs[dim.half :]
    n, e = dim.ndof, dim.elem
    gather_parts(dim, place, parts, solved)
    precon[...] = smooth[...]
    coarse_add(dim, solved[...], my, hot2, precon)
    consts = (visc, fric, lap, g3, gs)
    second_step(dim, resid, search, precon, scal, consts, v3, uy, image)
    mine = pl.ds(pl.multiple_of(place[4] * e, e), e)
    iterate[...] = precon[:, mine]
    for index in range(dim.parts):
        ref, start = block_of(dim, own, partner, n, index)
        columns = pl.ds(pl.multiple_of(place[4 + index] * e, e), e)
        source[:, columns] = ref[start : start + n, :] * precon[:, columns]
    group_solve(dim, place, source, hot_own, m3t, inv_own, inv_partner, out)


def adjoint_kernel(
    dim, place, smooth, source, visc, fric, lap, g3, gs, hot2, my, m3t, hot_own, inv_own,
    inv_partner, *refs,
):
    parts = refs[: dim.half]
    search, resid, scal, out, v3, uy, image, solved = refs[dim.half :]
    gather_parts(dim, place, parts, solved)
    search[...] = smooth[...]
    coarse_add(dim, solved[...], my, hot2, search)
    consts = (visc, fric, lap, g3, gs)
    first_step(dim, source, None, image, consts, v3, uy, resid, search, scal)
    group_solve(dim, place, resid, hot_own, m3t, inv_own, inv_partner, out)


def final_kernel(
    dim, place, smooth, resid, search, scal, source, sens, visc, fric, lap, g3, gs, hot2, my, *refs
):
    parts = refs[: dim.half]
    action, trace, v3, uy, image, solved, precon = refs[dim.half :]
    e = dim.elem
    gather_parts(dim, place, parts, solved)
    precon[...] = smooth[...]
    coarse_add(dim, solved[...], my, hot2, precon)
    consts = (visc, fric, lap, g3, gs)
    second_step(dim, resid, search, precon, scal, consts, v3, uy, image)
    mine = pl.ds(pl.multiple_of(place[4] * e, e), e)
    action[...] = sens[...] * precon[:, mine]
    trace[...] = jnp.broadcast_to(total(source[...] * precon[...]), (1, 128))


def replicated(
    probes,
    viscosity,
    friction,
    sensitivity,
    misfit_weight,
    grad_ref,
    trace_ref,
    coarse_modes,
    coarse_inv,
    peer_slots,
    local_pairs,
    elem_agg,
):
    leaf_count = lax.axis_size("leaf")
    dim = Dims(
        viscosity.shape[0],
        viscosity.shape[1],
        2 * leaf_count,
        peer_slots.shape[2],
        coarse_modes.shape[1],
        coarse_inv.shape[0],
    )
    n, e, ne = dim.ndof, dim.elem, dim.total
    leaf, agg = lax.axis_index("leaf"), lax.axis_index("agg")
    order = jnp.arange(dim.half, dtype=jnp.int32)
    chips = leaf ^ order
    place = jnp.concatenate(
        [
            jnp.stack([leaf, agg, leaf, agg]),
            chips * 2 + agg,
            chips * 2 + (1 - agg),
        ]
    ).astype(jnp.int32)
    flip = [(0, 1), (1, 0)]

    def to_partner(value):
        return lax.ppermute(value, "agg", flip)

    def peers(value):
        found = [value]
        for step in range(1, leaf_count):
            pairs = [(index, index ^ step) for index in range(leaf_count)]
            found.append(lax.ppermute(value, "leaf", pairs))
        return found

    def gather(value):
        own = jnp.concatenate(peers(value), axis=0)
        return own, to_partner(own)

    rows = jnp.concatenate(
        [
            local_pairs.astype(f32),
            peer_slots.reshape(1, e).astype(f32),
            elem_agg.reshape(1, e).astype(f32),
            jnp.zeros((4, e), f32),
        ],
        axis=0,
    )
    g3, gs, gsq3, my, m3t, trsq = prepare(dim, grad_ref, trace_ref, coarse_modes)
    source_own, sums = call(
        lambda *refs: source_kernel(dim, *refs),
        "source",
        [((n, e), f32), ((dim.modes, dim.group), f32)],
        [place, probes[0], sensitivity, elem_agg.reshape(1, e).astype(f32), m3t],
        [SM, VM, VM, VM, VM],
    )
    own_a, partner_a = gather(jnp.concatenate([source_own, rows], axis=0))
    inv_partner = to_partner(coarse_inv)
    (solved_own,) = call(
        lambda *refs: source_coarse_kernel(dim, *refs),
        "source_coarse",
        [((dim.aggs, dim.modes), f32)],
        [place, sums, to_partner(sums), coarse_inv],
        [SM, VM, VM, VM],
    )
    own_b, partner_b = gather(jnp.concatenate([viscosity, friction, solved_own], axis=0))
    own_c, partner_c = gather(misfit_weight)

    field = ((n, ne), f32)
    source, lap, hot2, counts, hot_own = call(
        lambda *refs: build_kernel(dim, *refs),
        "build",
        [
            field,
            ((ne, ne), bf16),
            ((dim.all_aggs, ne), bf16),
            ((1, ne), f32),
            ((dim.group, 2 * e), bf16),
        ],
        [place, own_a, partner_a],
        [SM, VM, VM],
        scratch=[VM((dim.parts, e), f32), VM((2 * dim.parts, e), f32), VM((1, ne), f32)],
    )
    work = [VM((3 * n, ne), bf16), VM((6 * n, ne), bf16)]
    image = VM((n, ne), f32)
    solved = VM((dim.all_aggs, dim.modes), f32)
    scal_shape = ((8, 128), f32)
    out_shape = ((dim.group, dim.modes), f32)
    once = 2 * ne * n * (9 * n + 2 * ne)

    visc, fric, w_diag, search, resid, scal, out = call(
        lambda *refs: forward_kernel(dim, *refs),
        "forward",
        [field] * 5 + [scal_shape, out_shape],
        [place, own_b, partner_b, source, counts, trsq, lap, g3, gs, gsq3, hot2, my, m3t]
        + [hot_own, coarse_inv, inv_partner],
        [SM] + [VM] * 15,
        scratch=work + [image, solved],
        flops=3 * once,
    )

    def smooth_of(value):
        (found,) = call(
            lambda *refs: smooth_kernel(dim, *refs),
            "smooth",
            [field],
            [value, visc, fric, w_diag, lap, g3, gs],
            scratch=work,
            flops=2 * once,
        )
        return found

    parts = peers(out)
    smooth = smooth_of(resid)
    iterate, source_two, out = call(
        lambda *refs: middle_kernel(dim, *refs),
        "middle",
        [((n, e), f32), field, out_shape],
        [place, smooth, resid, search, scal, own_c, partner_c, visc, fric, lap, g3, gs, hot2, my]
        + [m3t, hot_own, coarse_inv, inv_partner]
        + parts,
        [SM] + [VM] * (17 + dim.half),
        scratch=work + [image, solved, image],
        flops=once,
    )
    parts = peers(out)
    smooth = smooth_of(source_two)
    search, resid, scal, out = call(
        lambda *refs: adjoint_kernel(dim, *refs),
        "adjoint",
        [field, field, scal_shape, out_shape],
        [place, smooth, source_two, visc, fric, lap, g3, gs, hot2, my, m3t, hot_own, coarse_inv]
        + [inv_partner]
        + parts,
        [SM] + [VM] * (13 + dim.half),
        scratch=work + [image, solved],
        flops=once,
    )
    parts = peers(out)
    smooth = smooth_of(resid)
    action, trace = call(
        lambda *refs: final_kernel(dim, *refs),
        "final",
        [((n, e), f32), ((1, 128), f32)],
        [place, smooth, resid, search, scal, source, sensitivity, visc, fric, lap, g3, gs, hot2]
        + [my]
        + parts,
        [SM] + [VM] * (13 + dim.half),
        scratch=work + [image, solved, image],
        flops=once,
    )
    trace_value = lax.psum(trace[0, 0], "probe") / lax.axis_size("probe")
    return iterate[None], action[None], trace_value


def fits_one_core(mesh, viscosity, coarse_modes, coarse_inv, peer_slots, local_pairs):
    leaf_count, agg_count = mesh.shape["leaf"], mesh.shape["agg"]
    ndof, elem = viscosity.shape
    parts = leaf_count * agg_count
    cap = peer_slots.shape[2]
    aggs = coarse_inv.shape[0]
    return (
        agg_count == 2
        and leaf_count & (leaf_count - 1) == 0
        and elem == 128
        and coarse_modes.shape[1] == 128
        and parts * cap == elem
        and local_pairs.shape[1] == elem
        and ndof % 16 == 0
        and aggs % 8 == 0
        and local_pairs.shape[1] + (parts - 1) * cap <= 256
        and parts * elem <= 1024
    )


def solution(mesh):
    in_specs = (
        P("probe", None, ("leaf", "agg")),
        P(None, ("leaf", "agg")),
        P(None, ("leaf", "agg")),
        P(None, ("leaf", "agg")),
        P(None, ("leaf", "agg")),
        P(),
        P(),
        P(),
        P(("leaf", "agg"), None, None),
        P(("leaf", "agg"), None, None),
        P(None, ("leaf", "agg")),
        P(("leaf", "agg")),
    )
    out_specs = (P("probe", None, ("leaf", "agg")), P("probe", None, ("leaf", "agg")), P())

    def on_device(*args):
        if fits_one_core(mesh, args[1], args[7], args[8], args[9], args[10]):
            return replicated(*args)
        return distributed(*args)

    return jax.shard_map(
        on_device, mesh=mesh, in_specs=in_specs, out_specs=out_specs, check_vma=False
    )
```

```python
import jax
import jax.numpy as jnp
from jax import lax
from jax.experimental import pallas as pl
from jax.experimental.pallas import tpu as pltpu
from jax.sharding import PartitionSpec as P

ITERS = 2
SWEEPS = 3


highest = lax.Precision.HIGHEST
relax_weight = 0.6
f32 = jnp.float32
bf16 = jnp.bfloat16


def matmul(left, right):
    return jnp.dot(left, right, precision=highest, preferred_element_type=jnp.float32)


def distributed(
    probes,
    viscosity,
    friction,
    sensitivity,
    misfit_weight,
    grad_ref,
    trace_ref,
    coarse_modes,
    coarse_inv,
    peer_slots,
    local_pairs,
    elem_agg,
):
    agg_count = lax.axis_size("agg")
    elem_local = viscosity.shape[1]
    slot_flat = peer_slots.reshape(-1)
    filled = slot_flat >= 0
    own_local = jnp.where(filled, slot_flat, 0)
    filled_float = filled.astype(jnp.float32)
    first_end = local_pairs[0]
    second_end = local_pairs[1]
    counts = jnp.zeros((elem_local,), jnp.float32)
    counts = counts.at[first_end].add(1.0).at[second_end].add(1.0).at[own_local].add(filled_float)
    trace_square = jnp.sum(trace_ref * trace_ref, axis=0)
    diag_op = (
        matmul((grad_ref * grad_ref).T, viscosity)
        + friction
        + counts[None, :] * trace_square[:, None]
    )
    group_aggs = agg_count * coarse_inv.shape[0]
    one_hot = (elem_agg[:, None] == jnp.arange(group_aggs, dtype=jnp.int32)[None, :]).astype(
        jnp.float32
    )

    def operate(field_vec):
        inner_term = matmul(grad_ref.T, viscosity * matmul(grad_ref, field_vec))
        traces = matmul(trace_ref, field_vec)
        outgoing = traces[:, own_local] * filled_float[None, :]
        incoming = lax.all_to_all(
            outgoing, ("leaf", "agg"), split_axis=1, concat_axis=1, tiled=True
        )
        cross_diff = outgoing - incoming
        local_diff = traces[:, first_end] - traces[:, second_end]
        accumulated = jnp.zeros_like(field_vec)
        accumulated = (
            accumulated.at[:, first_end].add(local_diff).at[:, second_end].add(-local_diff)
        )
        accumulated = accumulated.at[:, own_local].add(cross_diff)
        return inner_term + friction * field_vec + matmul(trace_ref.T, accumulated)

    def coarse(residual_now):
        projected = matmul(coarse_modes.T, residual_now)
        coarse_sums = matmul(projected, one_hot)
        own_sums = lax.psum_scatter(coarse_sums, "agg", scatter_dimension=1, tiled=True)
        solved_own = jnp.einsum("acd,da->ca", coarse_inv, own_sums, precision=highest)
        solved_all = lax.all_gather(solved_own, "agg", axis=1, tiled=True)
        return matmul(coarse_modes, matmul(solved_all, one_hot.T))

    def precond(residual_now):
        smooth = relax_weight * residual_now / diag_op
        for sweep_index in range(SWEEPS - 1):
            smooth = smooth + relax_weight * (residual_now - operate(smooth)) / diag_op
        return smooth + coarse(residual_now)

    def energy_sum(left, right):
        return lax.psum(jnp.sum(left * right), ("leaf", "agg"))

    def krylov(source):
        residual_now = source
        precon = precond(residual_now)
        search = precon
        energy_now = energy_sum(residual_now, precon)
        iterate = jnp.zeros_like(source)
        for iteration in range(ITERS):
            image_vec = operate(search)
            step_size = energy_now / lax.psum(jnp.sum(search * image_vec), ("leaf", "agg"))
            iterate = iterate + step_size * search
            if iteration + 1 < ITERS:
                residual_now = residual_now - step_size * image_vec
                precon = precond(residual_now)
                energy_next = energy_sum(residual_now, precon)
                search = precon + energy_next / energy_now * search
                energy_now = energy_next
        return iterate

    probe_field = probes[0]
    forward = krylov(sensitivity * probe_field)
    adjoint = krylov(misfit_weight * forward)
    action = sensitivity * adjoint
    trace_value = lax.psum(jnp.sum(probe_field * action), ("leaf", "agg", "probe")) / lax.axis_size(
        "probe"
    )
    return (forward[None], action[None], trace_value)


def split(value):
    high = value.astype(bf16)
    low = (value - high.astype(f32)).astype(bf16)
    return high, low


def dot(left, right):
    return jnp.dot(left, right, preferred_element_type=f32)


def dot_nt(left, right):
    return lax.dot_general(left, right, (((1,), (1,)), ((), ())), preferred_element_type=f32)


def total(value):
    return jnp.sum(jnp.sum(value, axis=0, keepdims=True), axis=1, keepdims=True)


def spec(space):
    return pl.BlockSpec(memory_space=space)


VM = pltpu.VMEM
SM = pltpu.SMEM


def call(kernel, name, outs, args, spaces=None, scratch=(), flops=0, bytes_accessed=0):
    spaces = spaces or [VM] * len(args)
    return pl.pallas_call(
        kernel,
        name=name,
        out_shape=[jax.ShapeDtypeStruct(*one) for one in outs],
        in_specs=[spec(space) for space in spaces],
        out_specs=[spec(VM) for _ in outs],
        scratch_shapes=list(scratch),
        compiler_params=pltpu.CompilerParams(vmem_limit_bytes=16 * 1024 * 1024),
        cost_estimate=pl.CostEstimate(
            flops=flops, bytes_accessed=bytes_accessed, transcendentals=0
        ),
    )(*args)


class Dims:
    def __init__(self, ndof, elem, parts, cap, modes, aggs):
        self.ndof, self.elem, self.parts, self.cap = ndof, elem, parts, cap
        self.modes, self.aggs = modes, aggs
        self.total = elem * parts
        self.half = parts // 2
        self.group = 2 * aggs
        self.all_aggs = parts * aggs
        self.chunk = 2 * elem


def prepare_kernel(dim, grad, trace, modes, g3, gs, gsq3, my, m3t, trsq):
    n = dim.ndof
    high, low = split(grad[...])
    g3[:, 0:n], g3[:, n : 2 * n], g3[:, 2 * n :] = high, high, low
    gt = grad[...].T
    tt = trace[...].T
    gram = lax.dot_general(
        tt, tt, (((1,), (1,)), ((), ())), precision=highest, preferred_element_type=f32
    )
    gh, gl = split(gt)
    sh, sl = split(gram)
    for place, piece in enumerate((gh, sh, gh, sh, gl, sl)):
        gs[:, place * n : (place + 1) * n] = piece
    qh, ql = split(gt * gt)
    gsq3[:, 0:n], gsq3[:, n : 2 * n], gsq3[:, 2 * n :] = qh, qh, ql
    mh, ml = split(modes[...])
    w = dim.modes
    my[:, 0:w], my[:, w : 2 * w], my[:, 2 * w :] = mh, mh, ml
    th, tl = split(modes[...].T)
    m3t[:, 0:n], m3t[:, n : 2 * n], m3t[:, 2 * n :] = th, th, tl
    trsq[...] = jnp.sum(tt * tt, axis=1, keepdims=True)


def prepare(dim, grad_ref, trace_ref, coarse_modes):
    n, w = dim.ndof, dim.modes
    return call(
        lambda *refs: prepare_kernel(dim, *refs),
        "prepare",
        [
            ((n, 3 * n), bf16),
            ((n, 6 * n), bf16),
            ((n, 3 * n), bf16),
            ((n, 3 * w), bf16),
            ((w, 3 * n), bf16),
            ((n, 1), f32),
        ],
        [grad_ref, trace_ref, coarse_modes],
        flops=10**8,
        bytes_accessed=10**6,
    )


def restrict(dim, field, hot, m3t):
    high, low = split(field)
    sums = dot_nt(high, hot) + dot_nt(low, hot)
    high, low = split(sums)
    return dot(m3t[...], jnp.concatenate([high, low, high], axis=0))


def solve_blocks(sums, first, inv, count):
    rows = []
    for index in range(count):
        column = sums[:, first + index : first + index + 1]
        rows.append(jnp.sum(inv[index] * column, axis=0, keepdims=True))
    return jnp.concatenate(rows, axis=0)


def hot_of(dim, agg_row, agg_index, columns):
    place = lax.broadcasted_iota(jnp.int32, (dim.group, columns), 0)
    wanted = lax.rem(place + agg_index * dim.aggs, dim.group)
    return jnp.where(wanted.astype(f32) == agg_row, 1.0, 0.0).astype(bf16)


def source_kernel(dim, place, probe, sens, agg_row, m3t, source, sums):
    value = probe[...] * sens[...]
    source[...] = value
    hot = hot_of(dim, agg_row[...], 0, dim.elem)
    sums[...] = restrict(dim, value, hot, m3t)


def source_coarse_kernel(dim, place, sums_own, sums_partner, inv_own, inv_partner, out):
    agg = place[1]
    sums = sums_own[...] + sums_partner[...]
    first, second = sums[:, 0 : dim.aggs], sums[:, dim.aggs :]
    mine = jnp.where(agg == 0, first, second)
    theirs = jnp.where(agg == 0, second, first)
    out[pl.ds(pl.multiple_of(agg * dim.aggs, dim.aggs), dim.aggs), :] = solve_blocks(
        mine, 0, inv_own, dim.aggs
    )
    out[pl.ds(pl.multiple_of((1 - agg) * dim.aggs, dim.aggs), dim.aggs), :] = solve_blocks(
        theirs, 0, inv_partner, dim.aggs
    )


def build_kernel(dim, place, *refs):
    blocks = refs[: dim.parts]
    source, lap, hot2, counts, hot_own, table, sides, agg = refs[dim.parts :]
    n, e = dim.ndof, dim.elem
    start = 0
    for index, ref in enumerate(blocks):
        where = place[4 + index]
        columns = pl.ds(pl.multiple_of(where * e, e), e)
        source[:, columns] = ref[start : start + n, :]
        sides[pl.ds(where, 1), :] = ref[start + n : start + n + 1, :]
        sides[pl.ds(where + dim.parts, 1), :] = ref[start + n + 1 : start + n + 2, :]
        table[pl.ds(where, 1), :] = ref[start + n + 2 : start + n + 3, :]
        group = (where // 2) * dim.group
        agg[:, columns] = ref[start + n + 3 : start + n + 4, :] + group.astype(f32)
    elem_id = lax.broadcasted_iota(jnp.int32, (e, e), 0).astype(f32)
    lane = lax.broadcasted_iota(jnp.int32, (e, e), 1)
    column_id = lax.broadcasted_iota(jnp.int32, (e, e), 1)
    row_id = lax.broadcasted_iota(jnp.int32, (e, e), 0)
    on_diagonal = row_id == column_id
    full = table[...]
    rolled = [full]
    for shift in range(1, dim.parts):
        rolled.append(pltpu.roll(full, shift * dim.cap, 1))
    slot_block = lane // dim.cap
    for p in range(dim.parts):
        mine = jnp.where(full[p : p + 1, :] == elem_id, 1.0, 0.0).astype(bf16)
        first = jnp.where(sides[p : p + 1, :] == elem_id, 1.0, 0.0)
        second = jnp.where(sides[p + dim.parts : p + dim.parts + 1, :] == elem_id, 1.0, 0.0)
        edge = (first - second).astype(bf16)
        local = dot_nt(edge, edge)
        count = jnp.sum(mine.astype(f32), axis=1, keepdims=True)
        for q in range(dim.parts):
            if q == p:
                block = local + jnp.where(on_diagonal, count, 0.0)
                diagonal = jnp.where(on_diagonal, block, 0.0)
                counts[:, p * e : (p + 1) * e] = jnp.sum(diagonal, axis=0, keepdims=True)
            else:
                row = rolled[(q - p) % dim.parts][q : q + 1, :]
                theirs = jnp.where((row == elem_id) & (slot_block == q), 1.0, 0.0).astype(bf16)
                block = -dot_nt(mine, theirs)
            lap[p * e : (p + 1) * e, q * e : (q + 1) * e] = block.astype(bf16)
    agg_id = lax.broadcasted_iota(jnp.int32, (dim.all_aggs, dim.total), 0).astype(f32)
    hot2[...] = jnp.where(agg[...] == agg_id, 1.0, 0.0).astype(bf16)
    leaf = place[0]
    span = 2 * e
    own_row = agg[:, pl.ds(pl.multiple_of(leaf * span, span), span)]
    own_row = own_row - (leaf * dim.group).astype(f32)
    hot_own[...] = hot_of(dim, own_row, place[1], span)


def chunks(dim):
    return [slice(start, start + dim.chunk) for start in range(0, dim.total, dim.chunk)]


def apply_operator(dim, vec, consts, v3, uy, emit):
    visc, fric, lap, g3, gs = consts
    n = dim.ndof
    for c in chunks(dim):
        high, low = split(vec[:, c])
        v3[0:n, c] = high
        v3[n : 2 * n, c] = low
        v3[2 * n : 3 * n, c] = high
    for c in chunks(dim):
        high, low = split(visc[:, c] * dot(g3[...], v3[:, c]))
        uy[0:n, c] = high
        uy[2 * n : 3 * n, c] = low
        uy[4 * n : 5 * n, c] = high
    for c in chunks(dim):
        both = dot(v3[0 : 2 * n, :], lap[:, c])
        high, low = split(both[0:n] + both[n : 2 * n])
        uy[n : 2 * n, c] = high
        uy[3 * n : 4 * n, c] = low
        uy[5 * n : 6 * n, c] = high
    for c in chunks(dim):
        emit(c, dot(gs[...], uy[:, c]) + fric[:, c] * vec[:, c])


def smooth_loop(dim, resid, smooth, w_diag, consts, v3, uy, nxt):
    for c in chunks(dim):
        smooth[:, c] = w_diag[:, c] * resid[:, c]

    def sweep(index, carry):
        def emit(c, image):
            smooth[:, c] = smooth[:, c] + w_diag[:, c] * (resid[:, c] - image)

        apply_operator(dim, smooth, consts, v3, uy, emit)
        return carry

    lax.fori_loop(0, SWEEPS - 1, sweep, 0)


def coarse_add(dim, solved, my, hot2, target):
    high, low = split(solved)
    coarse = dot_nt(my[...], jnp.concatenate([high, low, high], axis=1))
    high, low = split(coarse)
    for c in chunks(dim):
        target[:, c] = target[:, c] + dot(high, hot2[:, c]) + dot(low, hot2[:, c])


def group_solve(dim, place, resid, hot_own, m3t, inv_own, inv_partner, out):
    leaf, agg = place[0], place[1]
    span = 2 * dim.elem
    field = resid[:, pl.ds(pl.multiple_of(leaf * span, span), span)]
    sums = restrict(dim, field, hot_own[...], m3t)
    out[pl.ds(pl.multiple_of(agg * dim.aggs, dim.aggs), dim.aggs), :] = solve_blocks(
        sums, 0, inv_own, dim.aggs
    )
    out[pl.ds(pl.multiple_of((1 - agg) * dim.aggs, dim.aggs), dim.aggs), :] = solve_blocks(
        sums, dim.aggs, inv_partner, dim.aggs
    )


def first_step(dim, source, smooth, image, consts, v3, uy, resid, search, scal):
    n = dim.ndof

    def emit(c, value):
        image[:, c] = value

    apply_operator(dim, search, consts, v3, uy, emit)
    energy = total(source[...] * search[...])
    step = energy / total(search[...] * image[...])
    resid[...] = source[...] - step * image[...]
    scal[0:1, :] = jnp.broadcast_to(energy, (1, 128))
    scal[1:2, :] = jnp.broadcast_to(step, (1, 128))


def second_step(dim, resid, search, precon, scal, consts, v3, uy, image):
    energy = total(resid[...] * precon[...])
    ratio = energy / scal[0:1, 0:1]
    precon[...] = precon[...] + ratio * search[...]

    def emit(c, value):
        image[:, c] = value

    apply_operator(dim, precon, consts, v3, uy, emit)
    step = energy / total(precon[...] * image[...])
    precon[...] = scal[1:2, 0:1] * search[...] + step * precon[...]


def gather_parts(dim, place, parts, solved):
    for index, ref in enumerate(parts):
        where = place[4 + index] // 2
        solved[pl.ds(pl.multiple_of(where * dim.group, dim.group), dim.group), :] = ref[...]


def begin_kernel(dim, place, source, counts, trsq, lap, g3, gs, gsq3, *refs):
    e = dim.elem
    visc_blocks = refs[: dim.parts]
    fric_blocks = refs[dim.parts : 2 * dim.parts]
    visc, fric, w_diag, smooth, v3, uy = refs[2 * dim.parts :]
    for index in range(dim.parts):
        columns = pl.ds(pl.multiple_of(place[4 + index] * e, e), e)
        visc[:, columns] = visc_blocks[index][...]
        fric[:, columns] = fric_blocks[index][...]
    for c in chunks(dim):
        high, low = split(visc[:, c])
        diag = dot(gsq3[...], jnp.concatenate([high, low, high], axis=0))
        diag = diag + fric[:, c] + counts[:, c] * trsq[...]
        w_diag[:, c] = relax_weight / diag
    smooth_loop(dim, source, smooth, w_diag, (visc, fric, lap, g3, gs), v3, uy, None)


def smooth_kernel(dim, resid, visc, fric, w_diag, lap, g3, gs, smooth, v3, uy):
    smooth_loop(dim, resid, smooth, w_diag, (visc, fric, lap, g3, gs), v3, uy, None)


def middle_kernel(
    dim, place, smooth, resid, search, scal, visc, fric, lap, g3, gs, hot2, my, m3t,
    hot_own, inv_own, inv_partner, *refs,
):
    parts = refs[: dim.half]
    weights = refs[dim.half : dim.half + dim.parts]
    iterate, source, out, v3, uy, image, solved, precon = refs[dim.half + dim.parts :]
    n, e = dim.ndof, dim.elem
    gather_parts(dim, place, parts, solved)
    precon[...] = smooth[...]
    coarse_add(dim, solved[...], my, hot2, precon)
    consts = (visc, fric, lap, g3, gs)
    second_step(dim, resid, search, precon, scal, consts, v3, uy, image)
    mine = pl.ds(pl.multiple_of(place[4] * e, e), e)
    iterate[...] = precon[:, mine]
    for index, ref in enumerate(weights):
        columns = pl.ds(pl.multiple_of(place[4 + index] * e, e), e)
        source[:, columns] = ref[...] * precon[:, columns]
    group_solve(dim, place, source, hot_own, m3t, inv_own, inv_partner, out)


def step_kernel(
    dim, place, smooth, source, visc, fric, lap, g3, gs, hot2, my, m3t, hot_own, inv_own,
    inv_partner, *refs,
):
    parts = refs[: dim.half]
    search, resid, scal, out, v3, uy, image, solved = refs[dim.half :]
    gather_parts(dim, place, parts, solved)
    search[...] = smooth[...]
    coarse_add(dim, solved[...], my, hot2, search)
    consts = (visc, fric, lap, g3, gs)
    first_step(dim, source, None, image, consts, v3, uy, resid, search, scal)
    group_solve(dim, place, resid, hot_own, m3t, inv_own, inv_partner, out)


def final_kernel(
    dim, place, smooth, resid, search, scal, source, sens, visc, fric, lap, g3, gs, hot2, my, *refs
):
    parts = refs[: dim.half]
    action, trace, v3, uy, image, solved, precon = refs[dim.half :]
    e = dim.elem
    gather_parts(dim, place, parts, solved)
    precon[...] = smooth[...]
    coarse_add(dim, solved[...], my, hot2, precon)
    consts = (visc, fric, lap, g3, gs)
    second_step(dim, resid, search, precon, scal, consts, v3, uy, image)
    mine = pl.ds(pl.multiple_of(place[4] * e, e), e)
    action[...] = sens[...] * precon[:, mine]
    trace[...] = jnp.broadcast_to(total(source[...] * precon[...]), (1, 128))


def replicated(
    probes,
    viscosity,
    friction,
    sensitivity,
    misfit_weight,
    grad_ref,
    trace_ref,
    coarse_modes,
    coarse_inv,
    peer_slots,
    local_pairs,
    elem_agg,
):
    leaf_count = lax.axis_size("leaf")
    dim = Dims(
        viscosity.shape[0],
        viscosity.shape[1],
        2 * leaf_count,
        peer_slots.shape[2],
        coarse_modes.shape[1],
        coarse_inv.shape[0],
    )
    n, e, ne = dim.ndof, dim.elem, dim.total
    leaf, agg = lax.axis_index("leaf"), lax.axis_index("agg")
    order = jnp.arange(dim.half, dtype=jnp.int32)
    chips = leaf ^ order
    place = jnp.concatenate(
        [
            jnp.stack([leaf, agg, leaf, agg]),
            chips * 2 + agg,
            chips * 2 + (1 - agg),
        ]
    ).astype(jnp.int32)
    flip = [(0, 1), (1, 0)]

    def to_partner(value):
        return lax.ppermute(value, "agg", flip)

    def peers(value):
        found = [value]
        for step in range(1, leaf_count):
            pairs = [(index, index ^ step) for index in range(leaf_count)]
            found.append(lax.ppermute(value, "leaf", pairs))
        return found

    def gather(value):
        own = peers(value)
        return own + [to_partner(one) for one in own]

    visc_blocks = gather(viscosity)
    rows = jnp.concatenate(
        [
            local_pairs.astype(f32),
            peer_slots.reshape(1, e).astype(f32),
            elem_agg.reshape(1, e).astype(f32),
            jnp.zeros((4, e), f32),
        ],
        axis=0,
    )
    g3, gs, gsq3, my, m3t, trsq = prepare(dim, grad_ref, trace_ref, coarse_modes)
    source_own, sums = call(
        lambda *refs: source_kernel(dim, *refs),
        "source",
        [((n, e), f32), ((dim.modes, dim.group), f32)],
        [place, probes[0], sensitivity, elem_agg.reshape(1, e).astype(f32), m3t],
        [SM, VM, VM, VM, VM],
    )
    source_blocks = gather(jnp.concatenate([source_own, rows], axis=0))
    fric_blocks = gather(friction)
    inv_partner = to_partner(coarse_inv)
    (out,) = call(
        lambda *refs: source_coarse_kernel(dim, *refs),
        "source_coarse",
        [((dim.group, dim.modes), f32)],
        [place, sums, to_partner(sums), coarse_inv, inv_partner],
        [SM, VM, VM, VM, VM],
    )
    parts = peers(out)
    weight_blocks = gather(misfit_weight)

    field = ((n, ne), f32)
    source, lap, hot2, counts, hot_own = call(
        lambda *refs: build_kernel(dim, *refs),
        "build",
        [
            field,
            ((ne, ne), bf16),
            ((dim.all_aggs, ne), bf16),
            ((1, ne), f32),
            ((dim.group, 2 * e), bf16),
        ],
        [place] + source_blocks,
        [SM] + [VM] * dim.parts,
        scratch=[VM((dim.parts, e), f32), VM((2 * dim.parts, e), f32), VM((1, ne), f32)],
    )
    work = [VM((3 * n, ne), bf16), VM((6 * n, ne), bf16)]
    image = VM((n, ne), f32)
    solved = VM((dim.all_aggs, dim.modes), f32)
    scal_shape = ((8, 128), f32)
    out_shape = ((dim.group, dim.modes), f32)
    once = 2 * ne * n * (9 * n + 2 * ne)

    visc, fric, w_diag, smooth = call(
        lambda *refs: begin_kernel(dim, *refs),
        "begin",
        [field] * 4,
        [place, source, counts, trsq, lap, g3, gs, gsq3] + visc_blocks + fric_blocks,
        [SM] + [VM] * (7 + 2 * dim.parts),
        scratch=work,
        flops=2 * once,
    )

    def smooth_of(value):
        (found,) = call(
            lambda *refs: smooth_kernel(dim, *refs),
            "smooth",
            [field],
            [value, visc, fric, w_diag, lap, g3, gs],
            scratch=work,
            flops=2 * once,
        )
        return found

    def step_of(smooth, start, parts):
        return call(
            lambda *refs: step_kernel(dim, *refs),
            "step",
            [field, field, scal_shape, out_shape],
            [place, smooth, start, visc, fric, lap, g3, gs, hot2, my, m3t, hot_own, coarse_inv]
            + [inv_partner]
            + parts,
            [SM] + [VM] * (13 + dim.half),
            scratch=work + [image, solved],
            flops=once,
        )

    search, resid, scal, out = step_of(smooth, source, parts)
    parts = peers(out)
    smooth = smooth_of(resid)
    iterate, source_two, out = call(
        lambda *refs: middle_kernel(dim, *refs),
        "middle",
        [((n, e), f32), field, out_shape],
        [place, smooth, resid, search, scal, visc, fric, lap, g3, gs, hot2, my]
        + [m3t, hot_own, coarse_inv, inv_partner]
        + parts
        + weight_blocks,
        [SM] + [VM] * (15 + dim.half + dim.parts),
        scratch=work + [image, solved, image],
        flops=once,
    )
    parts = peers(out)
    smooth = smooth_of(source_two)
    search, resid, scal, out = step_of(smooth, source_two, parts)
    parts = peers(out)
    smooth = smooth_of(resid)
    action, trace = call(
        lambda *refs: final_kernel(dim, *refs),
        "final",
        [((n, e), f32), ((1, 128), f32)],
        [place, smooth, resid, search, scal, source, sensitivity, visc, fric, lap, g3, gs, hot2]
        + [my]
        + parts,
        [SM] + [VM] * (13 + dim.half),
        scratch=work + [image, solved, image],
        flops=once,
    )
    trace_value = lax.psum(trace[0, 0], "probe") / lax.axis_size("probe")
    return iterate[None], action[None], trace_value


def fits_one_core(mesh, viscosity, coarse_modes, coarse_inv, peer_slots, local_pairs):
    leaf_count, agg_count = mesh.shape["leaf"], mesh.shape["agg"]
    ndof, elem = viscosity.shape
    parts = leaf_count * agg_count
    cap = peer_slots.shape[2]
    aggs = coarse_inv.shape[0]
    return (
        agg_count == 2
        and leaf_count & (leaf_count - 1) == 0
        and elem == 128
        and coarse_modes.shape[1] == 128
        and parts * cap == elem
        and local_pairs.shape[1] == elem
        and ndof % 16 == 0
        and aggs % 8 == 0
        and local_pairs.shape[1] + (parts - 1) * cap <= 256
        and parts * elem <= 1024
    )


def solution(mesh):
    in_specs = (
        P("probe", None, ("leaf", "agg")),
        P(None, ("leaf", "agg")),
        P(None, ("leaf", "agg")),
        P(None, ("leaf", "agg")),
        P(None, ("leaf", "agg")),
        P(),
        P(),
        P(),
        P(("leaf", "agg"), None, None),
        P(("leaf", "agg"), None, None),
        P(None, ("leaf", "agg")),
        P(("leaf", "agg")),
    )
    out_specs = (P("probe", None, ("leaf", "agg")), P("probe", None, ("leaf", "agg")), P())

    def on_device(*args):
        if fits_one_core(mesh, args[1], args[7], args[8], args[9], args[10]):
            return replicated(*args)
        return distributed(*args)

    return jax.shard_map(
        on_device, mesh=mesh, in_specs=in_specs, out_specs=out_specs, check_vma=False
    )
```

```python
import jax
import jax.numpy as jnp
from jax import lax
from jax.experimental import pallas as pl
from jax.experimental.pallas import tpu as pltpu
from jax.sharding import PartitionSpec as P


ITERS = 2
SWEEPS = 3


highest = lax.Precision.HIGHEST
relax_weight = 0.6
f32 = jnp.float32
bf16 = jnp.bfloat16


def matmul(left, right):
    return jnp.dot(left, right, precision=highest, preferred_element_type=jnp.float32)


def distributed(
    probes,
    viscosity,
    friction,
    sensitivity,
    misfit_weight,
    grad_ref,
    trace_ref,
    coarse_modes,
    coarse_inv,
    peer_slots,
    local_pairs,
    elem_agg,
):
    agg_count = lax.axis_size("agg")
    elem_local = viscosity.shape[1]
    slot_flat = peer_slots.reshape(-1)
    filled = slot_flat >= 0
    own_local = jnp.where(filled, slot_flat, 0)
    filled_float = filled.astype(jnp.float32)
    first_end = local_pairs[0]
    second_end = local_pairs[1]
    counts = jnp.zeros((elem_local,), jnp.float32)
    counts = counts.at[first_end].add(1.0).at[second_end].add(1.0).at[own_local].add(filled_float)
    trace_square = jnp.sum(trace_ref * trace_ref, axis=0)
    diag_op = (
        matmul((grad_ref * grad_ref).T, viscosity)
        + friction
        + counts[None, :] * trace_square[:, None]
    )
    group_aggs = agg_count * coarse_inv.shape[0]
    one_hot = (elem_agg[:, None] == jnp.arange(group_aggs, dtype=jnp.int32)[None, :]).astype(
        jnp.float32
    )

    def operate(field_vec):
        inner_term = matmul(grad_ref.T, viscosity * matmul(grad_ref, field_vec))
        traces = matmul(trace_ref, field_vec)
        outgoing = traces[:, own_local] * filled_float[None, :]
        incoming = lax.all_to_all(
            outgoing, ("leaf", "agg"), split_axis=1, concat_axis=1, tiled=True
        )
        cross_diff = outgoing - incoming
        local_diff = traces[:, first_end] - traces[:, second_end]
        accumulated = jnp.zeros_like(field_vec)
        accumulated = (
            accumulated.at[:, first_end].add(local_diff).at[:, second_end].add(-local_diff)
        )
        accumulated = accumulated.at[:, own_local].add(cross_diff)
        return inner_term + friction * field_vec + matmul(trace_ref.T, accumulated)

    def coarse(residual_now):
        projected = matmul(coarse_modes.T, residual_now)
        coarse_sums = matmul(projected, one_hot)
        own_sums = lax.psum_scatter(coarse_sums, "agg", scatter_dimension=1, tiled=True)
        solved_own = jnp.einsum("acd,da->ca", coarse_inv, own_sums, precision=highest)
        solved_all = lax.all_gather(solved_own, "agg", axis=1, tiled=True)
        return matmul(coarse_modes, matmul(solved_all, one_hot.T))

    def precond(residual_now):
        smooth = relax_weight * residual_now / diag_op
        for _ in range(SWEEPS - 1):
            smooth = smooth + relax_weight * (residual_now - operate(smooth)) / diag_op
        return smooth + coarse(residual_now)

    def energy_sum(left, right):
        return lax.psum(jnp.sum(left * right), ("leaf", "agg"))

    def krylov(source):
        residual_now = source
        precon = precond(residual_now)
        search = precon
        energy_now = energy_sum(residual_now, precon)
        iterate = jnp.zeros_like(source)
        for iteration in range(ITERS):
            image_vec = operate(search)
            step_size = energy_now / lax.psum(jnp.sum(search * image_vec), ("leaf", "agg"))
            iterate = iterate + step_size * search
            if iteration + 1 < ITERS:
                residual_now = residual_now - step_size * image_vec
                precon = precond(residual_now)
                energy_next = energy_sum(residual_now, precon)
                search = precon + energy_next / energy_now * search
                energy_now = energy_next
        return iterate

    probe_field = probes[0]
    forward = krylov(sensitivity * probe_field)
    adjoint = krylov(misfit_weight * forward)
    action = sensitivity * adjoint
    trace_value = lax.psum(jnp.sum(probe_field * action), ("leaf", "agg", "probe")) / lax.axis_size(
        "probe"
    )
    return (forward[None], action[None], trace_value)


def split(value):
    high = value.astype(bf16)
    low = (value - high.astype(f32)).astype(bf16)
    return high, low


def dot(left, right):
    return jnp.dot(left, right, preferred_element_type=f32)


def dot_nt(left, right):
    return lax.dot_general(left, right, (((1,), (1,)), ((), ())), preferred_element_type=f32)


def total(value):
    return jnp.sum(jnp.sum(value, axis=0, keepdims=True), axis=1, keepdims=True)


def spec(space):
    return pl.BlockSpec(memory_space=space)


VM = pltpu.VMEM
SM = pltpu.SMEM


def call(kernel, outs, args, spaces=None, scratch=(), flops=0, bytes_accessed=0):
    return kernel_call(kernel, outs, args, spaces, scratch, flops, bytes_accessed)


def kernel_call(kernel, outs, args, spaces, scratch, flops, bytes_accessed):
    spaces = spaces or [VM] * len(args)
    args = [
        pltpu.with_memory_space_constraint(arg, space) if space == pltpu.HBM else arg
        for arg, space in zip(args, spaces)
    ]
    return pl.pallas_call(
        kernel,
        out_shape=[jax.ShapeDtypeStruct(*one) for one in outs],
        in_specs=[spec(space) for space in spaces],
        out_specs=[spec(VM) for _ in outs],
        scratch_shapes=list(scratch),
        compiler_params=pltpu.CompilerParams(vmem_limit_bytes=16 * 1024 * 1024),
        cost_estimate=pl.CostEstimate(
            flops=flops, bytes_accessed=bytes_accessed, transcendentals=0
        ),
    )(*args)


class Dims:
    def __init__(self, ndof, elem, parts, cap, modes, aggs):
        self.ndof, self.elem, self.parts, self.cap = ndof, elem, parts, cap
        self.modes, self.aggs = modes, aggs
        self.total = elem * parts
        self.half = parts // 2
        self.group = 2 * aggs
        self.all_aggs = parts * aggs
        self.chunk = 2 * elem


def prepare_constants(dim, grad, trace, modes, g3, gs, gsq3, my, m3t, trsq):
    n = dim.ndof
    high, low = split(grad)
    g3[:, 0:n], g3[:, n : 2 * n], g3[:, 2 * n :] = high, high, low
    gt = grad.T
    tt = trace.T
    gram = lax.dot_general(
        tt, tt, (((1,), (1,)), ((), ())), precision=highest, preferred_element_type=f32
    )
    gh, gl = split(gt)
    sh, sl = split(gram)
    for place, piece in enumerate((gh, sh, gh, sh, gl, sl)):
        gs[:, place * n : (place + 1) * n] = piece
    qh, ql = split(gt * gt)
    gsq3[:, 0:n], gsq3[:, n : 2 * n], gsq3[:, 2 * n :] = qh, qh, ql
    mh, ml = split(modes)
    w = dim.modes
    my[:, 0:w], my[:, w : 2 * w], my[:, 2 * w :] = mh, mh, ml
    th, tl = split(modes.T)
    m3t[:, 0:n], m3t[:, n : 2 * n], m3t[:, 2 * n :] = th, th, tl
    trsq[...] = jnp.sum(tt * tt, axis=1, keepdims=True)


def restrict(field, hot, m3t):
    high, low = split(field)
    sums = dot_nt(high, hot) + dot_nt(low, hot)
    high, low = split(sums)
    return dot(m3t[...], jnp.concatenate([high, low, high], axis=0))


def solve_blocks(sums, first, inv, count):
    rows = []
    for index in range(count):
        column = sums[:, first + index : first + index + 1]
        rows.append(jnp.sum(inv[index] * column, axis=0, keepdims=True))
    return jnp.concatenate(rows, axis=0)


def hot_of(dim, agg_row, agg_index, columns):
    place = lax.broadcasted_iota(jnp.int32, (dim.group, columns), 0)
    wanted = lax.rem(place + agg_index * dim.aggs, dim.group)
    return jnp.where(wanted.astype(f32) == agg_row, 1.0, 0.0).astype(bf16)


def source_kernel(
    dim, probe_in, sens_in, pairs_in, slots_in, agg_in, grad_in, trace_in, modes_in, inv_in,
    visc_in, payload, sums, g3, gs, gsq3, my, m3t, trsq, inv,
    probe, sens, pairs, slots, agg_row, grad, trace, modes, sems,
):
    moves = (
        (probe_in.at[0], probe),
        (sens_in, sens),
        (pairs_in, pairs),
        (slots_in.at[0], slots),
        (agg_in, agg_row),
        (grad_in, grad),
        (trace_in, trace),
        (modes_in, modes),
        (inv_in, inv),
        (visc_in, payload.at[pl.ds(dim.ndof + 8, dim.ndof)]),
    )
    copies = [
        pltpu.make_async_copy(src, dst, sems.at[index]) for index, (src, dst) in enumerate(moves)
    ]
    for copy in copies:
        copy.start()
    for copy in copies:
        copy.wait()
    n = dim.ndof
    value = probe[...] * sens[...]
    payload[0:n, :] = value
    agg_float = agg_row[...].astype(f32)
    payload[n : n + 2, :] = pairs[...].astype(f32)
    for part in range(dim.parts):
        span = slice(part * dim.cap, (part + 1) * dim.cap)
        payload[n + 2 : n + 3, span] = slots[part : part + 1, :].astype(f32)
    payload[n + 3 : n + 4, :] = agg_float
    payload[n + 4 : n + 8, :] = jnp.zeros((4, dim.elem), f32)
    prepare_constants(dim, grad[...], trace[...], modes[...], g3, gs, gsq3, my, m3t, trsq)
    hot = hot_of(dim, agg_float, 0, dim.elem)
    sums[...] = restrict(value, hot, m3t)


def source_coarse_kernel(
    dim, place, sums_own, sums_partner, inv_own, inv_partner, fric_in, out, sem
):
    n = dim.ndof
    copy = pltpu.make_async_copy(fric_in, out.at[pl.ds(0, n)], sem)
    copy.start()
    agg = place[1]
    sums = sums_own[...] + sums_partner[...]
    first, second = sums[:, 0 : dim.aggs], sums[:, dim.aggs :]
    mine = jnp.where(agg == 0, first, second)
    theirs = jnp.where(agg == 0, second, first)
    out[pl.ds(pl.multiple_of(n + agg * dim.aggs, dim.aggs), dim.aggs), :] = solve_blocks(
        mine, 0, inv_own, dim.aggs
    )
    out[pl.ds(pl.multiple_of(n + (1 - agg) * dim.aggs, dim.aggs), dim.aggs), :] = solve_blocks(
        theirs, 0, inv_partner, dim.aggs
    )
    copy.wait()


def build_kernel(dim, place, *refs):
    blocks = refs[: dim.parts]
    source, visc, lap, hot2, counts, hot_own, table, sides, agg = refs[dim.parts :]
    n, e = dim.ndof, dim.elem
    for index, ref in enumerate(blocks):
        where = place[4 + index]
        columns = pl.ds(pl.multiple_of(where * e, e), e)
        source[:, columns] = ref[0:n, :]
        visc[:, columns] = ref[n + 8 : 2 * n + 8, :]
        sides[pl.ds(where, 1), :] = ref[n : n + 1, :]
        sides[pl.ds(where + dim.parts, 1), :] = ref[n + 1 : n + 2, :]
        table[pl.ds(where, 1), :] = ref[n + 2 : n + 3, :]
        group = (where // 2) * dim.group
        agg[:, columns] = ref[n + 3 : n + 4, :] + group.astype(f32)
    elem_id = lax.broadcasted_iota(jnp.int32, (e, e), 0).astype(f32)
    lane = lax.broadcasted_iota(jnp.int32, (e, e), 1)
    column_id = lax.broadcasted_iota(jnp.int32, (e, e), 1)
    row_id = lax.broadcasted_iota(jnp.int32, (e, e), 0)
    on_diagonal = row_id == column_id
    full = table[...]
    rolled = [full]
    for shift in range(1, dim.parts):
        rolled.append(pltpu.roll(full, shift * dim.cap, 1))
    slot_block = lane // dim.cap
    for p in range(dim.parts):
        mine = jnp.where(full[p : p + 1, :] == elem_id, 1.0, 0.0).astype(bf16)
        first = jnp.where(sides[p : p + 1, :] == elem_id, 1.0, 0.0)
        second = jnp.where(sides[p + dim.parts : p + dim.parts + 1, :] == elem_id, 1.0, 0.0)
        edge = (first - second).astype(bf16)
        local = dot_nt(edge, edge)
        count = jnp.sum(mine.astype(f32), axis=1, keepdims=True)
        for q in range(dim.parts):
            if q == p:
                block = local + jnp.where(on_diagonal, count, 0.0)
                diagonal = jnp.where(on_diagonal, block, 0.0)
                counts[:, p * e : (p + 1) * e] = jnp.sum(diagonal, axis=0, keepdims=True)
            else:
                row = rolled[(q - p) % dim.parts][q : q + 1, :]
                theirs = jnp.where((row == elem_id) & (slot_block == q), 1.0, 0.0).astype(bf16)
                block = -dot_nt(mine, theirs)
            lap[p * e : (p + 1) * e, q * e : (q + 1) * e] = block.astype(bf16)
    agg_id = lax.broadcasted_iota(jnp.int32, (dim.all_aggs, dim.total), 0).astype(f32)
    hot2[...] = jnp.where(agg[...] == agg_id, 1.0, 0.0).astype(bf16)
    leaf = place[0]
    span = 2 * e
    own_row = agg[:, pl.ds(pl.multiple_of(leaf * span, span), span)]
    own_row = own_row - (leaf * dim.group).astype(f32)
    hot_own[...] = hot_of(dim, own_row, place[1], span)


def chunks(dim):
    return [slice(start, start + dim.chunk) for start in range(0, dim.total, dim.chunk)]


def apply_operator(dim, vec, consts, v3, uy, emit):
    visc, fric, lap, g3, gs = consts
    n = dim.ndof
    for c in chunks(dim):
        high, low = split(vec[:, c])
        v3[0:n, c] = high
        v3[n : 2 * n, c] = low
        v3[2 * n : 3 * n, c] = high
    for c in chunks(dim):
        high, low = split(visc[:, c] * dot(g3[...], v3[:, c]))
        uy[0:n, c] = high
        uy[2 * n : 3 * n, c] = low
        uy[4 * n : 5 * n, c] = high
    for c in chunks(dim):
        both = dot(v3[0 : 2 * n, :], lap[:, c])
        high, low = split(both[0:n] + both[n : 2 * n])
        uy[n : 2 * n, c] = high
        uy[3 * n : 4 * n, c] = low
        uy[5 * n : 6 * n, c] = high
    for c in chunks(dim):
        emit(c, dot(gs[...], uy[:, c]) + fric[:, c] * vec[:, c])


def smooth_loop(dim, resid, smooth, w_diag, consts, v3, uy):
    for c in chunks(dim):
        smooth[:, c] = w_diag[:, c] * resid[:, c]

    def sweep(index, carry):
        def emit(c, image):
            smooth[:, c] = smooth[:, c] + w_diag[:, c] * (resid[:, c] - image)

        apply_operator(dim, smooth, consts, v3, uy, emit)
        return carry

    lax.fori_loop(0, SWEEPS - 1, sweep, 0)


def coarse_add(dim, solved, my, hot2, target):
    high, low = split(solved)
    coarse = dot_nt(my[...], jnp.concatenate([high, low, high], axis=1))
    high, low = split(coarse)
    for c in chunks(dim):
        target[:, c] = target[:, c] + dot(high, hot2[:, c]) + dot(low, hot2[:, c])


def group_solve(dim, place, resid, hot_own, m3t, inv_own, inv_partner, out):
    leaf, agg = place[0], place[1]
    span = 2 * dim.elem
    field = resid[:, pl.ds(pl.multiple_of(leaf * span, span), span)]
    sums = restrict(field, hot_own[...], m3t)
    out[pl.ds(pl.multiple_of(agg * dim.aggs, dim.aggs), dim.aggs), :] = solve_blocks(
        sums, 0, inv_own, dim.aggs
    )
    out[pl.ds(pl.multiple_of((1 - agg) * dim.aggs, dim.aggs), dim.aggs), :] = solve_blocks(
        sums, dim.aggs, inv_partner, dim.aggs
    )


def first_step(dim, source, image, consts, v3, uy, resid, search, scal):
    def emit(c, value):
        image[:, c] = value

    apply_operator(dim, search, consts, v3, uy, emit)
    energy = total(source[...] * search[...])
    step = energy / total(search[...] * image[...])
    resid[...] = source[...] - step * image[...]
    scal[0:1, :] = jnp.broadcast_to(energy, (1, 128))
    scal[1:2, :] = jnp.broadcast_to(step, (1, 128))


def second_step(dim, resid, search, precon, scal, consts, v3, uy, image):
    energy = total(resid[...] * precon[...])
    ratio = energy / scal[0:1, 0:1]
    precon[...] = precon[...] + ratio * search[...]

    def emit(c, value):
        image[:, c] = value

    apply_operator(dim, precon, consts, v3, uy, emit)
    step = energy / total(precon[...] * image[...])
    precon[...] = scal[1:2, 0:1] * search[...] + step * precon[...]


def gather_parts(dim, place, parts, solved):
    groups = []
    for ref in parts:
        skip = ref.shape[0] % dim.ndof
        first = ref.shape[0] - skip
        groups += [(ref, first + step) for step in range(0, skip, dim.group)]
    for index, (ref, first) in enumerate(groups):
        where = place[4 + index] // 2
        solved[pl.ds(pl.multiple_of(where * dim.group, dim.group), dim.group), :] = ref[
            first : first + dim.group, :
        ]


def begin_kernel(dim, place, source, visc, counts, trsq, lap, g3, gs, gsq3, *refs):
    n, e = dim.ndof, dim.elem
    fric_blocks = refs[: dim.parts]
    fric, w_diag, smooth, v3, uy = refs[dim.parts :]
    for index in range(dim.parts):
        columns = pl.ds(pl.multiple_of(place[4 + index] * e, e), e)
        fric[:, columns] = fric_blocks[index][0:n, :]
    for c in chunks(dim):
        high, low = split(visc[:, c])
        diag = dot(gsq3[...], jnp.concatenate([high, low, high], axis=0))
        diag = diag + fric[:, c] + counts[:, c] * trsq[...]
        w_diag[:, c] = relax_weight / diag
    smooth_loop(dim, source, smooth, w_diag, (visc, fric, lap, g3, gs), v3, uy)


def sweep_kernel(dim, first, resid, visc, fric, w_diag, lap, g3, gs, *refs):
    if first:
        smooth, v3, uy, start = refs
        for c in chunks(dim):
            start[:, c] = w_diag[:, c] * resid[:, c]
    else:
        start, smooth, v3, uy = refs

    def emit(c, image):
        smooth[:, c] = start[:, c] + w_diag[:, c] * (resid[:, c] - image)

    apply_operator(dim, start, (visc, fric, lap, g3, gs), v3, uy, emit)


def middle_kernel(
    dim, place, smooth, resid, search, scal, visc, fric, lap, g3, gs, hot2, my, m3t,
    hot_own, inv_own, inv_partner, *refs,
):
    weights = refs[: dim.parts]
    parts = refs[dim.parts : -8]
    iterate, source, out, v3, uy, image, solved, precon = refs[-8:]
    e = dim.elem
    gather_parts(dim, place, parts, solved)
    precon[...] = smooth[...]
    coarse_add(dim, solved[...], my, hot2, precon)
    consts = (visc, fric, lap, g3, gs)
    second_step(dim, resid, search, precon, scal, consts, v3, uy, image)
    mine = pl.ds(pl.multiple_of(place[4] * e, e), e)
    iterate[...] = precon[:, mine]
    for index, ref in enumerate(weights):
        columns = pl.ds(pl.multiple_of(place[4 + index] * e, e), e)
        source[:, columns] = ref[...] * precon[:, columns]
    group_solve(dim, place, source, hot_own, m3t, inv_own, inv_partner, out)


def step_kernel(
    dim, place, smooth, source, visc, fric, lap, g3, gs, hot2, my, m3t, hot_own, inv_own,
    inv_partner, *refs,
):
    parts = refs[:-8]
    search, resid, scal, out, v3, uy, image, solved = refs[-8:]
    gather_parts(dim, place, parts, solved)
    search[...] = smooth[...]
    coarse_add(dim, solved[...], my, hot2, search)
    consts = (visc, fric, lap, g3, gs)
    first_step(dim, source, image, consts, v3, uy, resid, search, scal)
    group_solve(dim, place, resid, hot_own, m3t, inv_own, inv_partner, out)


def final_kernel(
    dim, place, smooth, resid, search, scal, source, sens, visc, fric, lap, g3, gs, hot2, my, *refs
):
    parts = refs[:-7]
    action, trace, v3, uy, image, solved, precon = refs[-7:]
    e = dim.elem
    gather_parts(dim, place, parts, solved)
    precon[...] = smooth[...]
    coarse_add(dim, solved[...], my, hot2, precon)
    consts = (visc, fric, lap, g3, gs)
    second_step(dim, resid, search, precon, scal, consts, v3, uy, image)
    mine = pl.ds(pl.multiple_of(place[4] * e, e), e)
    action[...] = sens[...] * precon[:, mine]
    trace[...] = jnp.broadcast_to(total(source[...] * precon[...]), (1, 128))


def replicated(
    probes,
    viscosity,
    friction,
    sensitivity,
    misfit_weight,
    grad_ref,
    trace_ref,
    coarse_modes,
    coarse_inv,
    peer_slots,
    local_pairs,
    elem_agg,
):
    leaf_count = lax.axis_size("leaf")
    dim = Dims(
        viscosity.shape[0],
        viscosity.shape[1],
        2 * leaf_count,
        peer_slots.shape[2],
        coarse_modes.shape[1],
        coarse_inv.shape[0],
    )
    n, e, ne = dim.ndof, dim.elem, dim.total
    leaf, agg = lax.axis_index("leaf"), lax.axis_index("agg")
    order = jnp.arange(dim.half, dtype=jnp.int32)
    chips = leaf ^ order
    place = jnp.concatenate(
        [
            jnp.stack([leaf, agg, leaf, agg]),
            chips * 2 + agg,
            chips * 2 + (1 - agg),
        ]
    ).astype(jnp.int32)
    flip = [(0, 1), (1, 0)]

    def to_partner(value):
        return lax.ppermute(value, "agg", flip)

    def peers(value):
        found = [value]
        for step in range(1, leaf_count):
            pairs = [(index, index ^ step) for index in range(leaf_count)]
            found.append(lax.ppermute(value, "leaf", pairs))
        return found

    def gather(value):
        own = peers(value)
        return own + [to_partner(one) for one in own]

    payload, sums, g3, gs, gsq3, my, m3t, trsq, inv_own = call(
        lambda *refs: source_kernel(dim, *refs),
        [
            ((2 * n + 8, e), f32),
            ((dim.modes, dim.group), f32),
            ((n, 3 * n), bf16),
            ((n, 6 * n), bf16),
            ((n, 3 * n), bf16),
            ((n, 3 * dim.modes), bf16),
            ((dim.modes, 3 * n), bf16),
            ((n, 1), f32),
            (coarse_inv.shape, f32),
        ],
        [probes, sensitivity, local_pairs, peer_slots, elem_agg.reshape(1, e)]
        + [grad_ref, trace_ref, coarse_modes, coarse_inv, viscosity],
        [pltpu.HBM] * 10,
        scratch=[
            VM((n, e), f32),
            VM((n, e), f32),
            VM((2, e), jnp.int32),
            VM((dim.parts, dim.cap), jnp.int32),
            VM((1, e), jnp.int32),
            VM((n, n), f32),
            VM((n, n), f32),
            VM((n, dim.modes), f32),
            pltpu.SemaphoreType.DMA((10,)),
        ],
        flops=10**8,
    )
    source_blocks = gather(payload)
    inv_partner = to_partner(inv_own)
    sums_partner = to_partner(sums)
    (second_payload,) = call(
        lambda *refs: source_coarse_kernel(dim, *refs),
        [((n + dim.group, e), f32)],
        [place, sums, sums_partner, inv_own, inv_partner, friction],
        [SM, VM, VM, VM, VM, pltpu.HBM],
        scratch=[pltpu.SemaphoreType.DMA(())],
    )
    parts = peers(second_payload)
    fric_blocks = parts + [to_partner(one) for one in parts]
    own = peers(misfit_weight)
    weight_blocks = own + [to_partner(one) for one in own]

    field = ((n, ne), f32)
    source, visc, lap, hot2, counts, hot_own = call(
        lambda *refs: build_kernel(dim, *refs),
        [
            field,
            field,
            ((ne, ne), bf16),
            ((dim.all_aggs, ne), bf16),
            ((1, ne), f32),
            ((dim.group, 2 * e), bf16),
        ],
        [place] + source_blocks,
        [SM] + [VM] * dim.parts,
        scratch=[VM((dim.parts, e), f32), VM((2 * dim.parts, e), f32), VM((1, ne), f32)],
    )
    work = [VM((3 * n, ne), bf16), VM((6 * n, ne), bf16)]
    image = VM((n, ne), f32)
    solved = VM((dim.all_aggs, dim.modes), f32)
    scal_shape = ((8, 128), f32)
    out_shape = ((dim.group, dim.modes), f32)
    once = 2 * ne * n * (9 * n + 2 * ne)

    fric, w_diag, smooth = call(
        lambda *refs: begin_kernel(dim, *refs),
        [field] * 3,
        [place, source, visc, counts, trsq, lap, g3, gs, gsq3] + fric_blocks,
        [SM] + [VM] * (8 + dim.parts),
        scratch=work,
        flops=2 * once,
    )

    def sweep_of(first, args):
        (found,) = call(
            lambda *refs: sweep_kernel(dim, first, *refs),
            [field],
            args,
            scratch=work + ([image] if first else []),
            flops=once,
        )
        return found

    def smooth_and_spread(value, solved_group):
        consts = [value, visc, fric, w_diag, lap, g3, gs]
        smooth, found = None, solved_group
        parts = [solved_group]
        for sweep in range(SWEEPS - 1):
            width = 2**sweep
            if width < leaf_count:
                pairs = [(index, index ^ width) for index in range(leaf_count)]
                other = lax.ppermute(found, "leaf", pairs)
                parts.append(other)
                if 2 * width < leaf_count:
                    found = jnp.concatenate([found, other], axis=0)
            smooth = sweep_of(sweep == 0, consts if sweep == 0 else consts + [smooth])
        return smooth, parts

    def step_of(smooth, start, parts):
        return call(
            lambda *refs: step_kernel(dim, *refs),
            [field, field, scal_shape, out_shape],
            [place, smooth, start, visc, fric, lap, g3, gs, hot2, my, m3t, hot_own, inv_own]
            + [inv_partner]
            + parts,
            [SM] + [VM] * (13 + len(parts)),
            scratch=work + [image, solved],
            flops=once,
        )

    search, resid, scal, out = step_of(smooth, source, parts)
    smooth, parts = smooth_and_spread(resid, out)
    iterate, source_two, out = call(
        lambda *refs: middle_kernel(dim, *refs),
        [((n, e), f32), field, out_shape],
        [place, smooth, resid, search, scal, visc, fric, lap, g3, gs, hot2, my]
        + [m3t, hot_own, inv_own, inv_partner]
        + weight_blocks
        + parts,
        [SM] + [VM] * (15 + dim.parts + len(parts)),
        scratch=work + [image, solved, image],
        flops=once,
    )
    smooth, parts = smooth_and_spread(source_two, out)
    search, resid, scal, out = step_of(smooth, source_two, parts)
    smooth, parts = smooth_and_spread(resid, out)
    action, trace = call(
        lambda *refs: final_kernel(dim, *refs),
        [((n, e), f32), ((1, 128), f32)],
        [place, smooth, resid, search, scal, source, sensitivity, visc, fric, lap, g3, gs, hot2]
        + [my]
        + parts,
        [SM] + [VM] * (13 + len(parts)),
        scratch=work + [image, solved, image],
        flops=once,
    )
    probe_count = lax.axis_size("probe")
    traces = [trace]
    for step in range(1, probe_count):
        pairs = [(index, (index + step) % probe_count) for index in range(probe_count)]
        if probe_count & (probe_count - 1) == 0:
            pairs = [(index, index ^ step) for index in range(probe_count)]
        traces.append(lax.ppermute(trace, "probe", pairs))
    trace_value = sum(one[0, 0] for one in traces) / probe_count
    return iterate[None], action[None], trace_value


def fits_one_core(mesh, viscosity, coarse_modes, coarse_inv, peer_slots, local_pairs):
    leaf_count, agg_count = mesh.shape["leaf"], mesh.shape["agg"]
    ndof, elem = viscosity.shape
    parts = leaf_count * agg_count
    cap = peer_slots.shape[2]
    aggs = coarse_inv.shape[0]
    return (
        agg_count == 2
        and leaf_count & (leaf_count - 1) == 0
        and leaf_count <= 2 ** (SWEEPS - 1)
        and elem == 128
        and coarse_modes.shape[1] == 128
        and parts * cap == elem
        and local_pairs.shape[1] == elem
        and ndof % 16 == 0
        and aggs % 8 == 0
        and local_pairs.shape[1] + (parts - 1) * cap <= 256
        and parts * elem <= 1024
    )


def solution(mesh):
    in_specs = (
        P("probe", None, ("leaf", "agg")),
        P(None, ("leaf", "agg")),
        P(None, ("leaf", "agg")),
        P(None, ("leaf", "agg")),
        P(None, ("leaf", "agg")),
        P(),
        P(),
        P(),
        P(("leaf", "agg"), None, None),
        P(("leaf", "agg"), None, None),
        P(None, ("leaf", "agg")),
        P(("leaf", "agg")),
    )
    out_specs = (P("probe", None, ("leaf", "agg")), P("probe", None, ("leaf", "agg")), P())

    def on_device(*args):
        if fits_one_core(mesh, args[1], args[7], args[8], args[9], args[10]):
            return replicated(*args)
        return distributed(*args)

    return jax.shard_map(
        on_device, mesh=mesh, in_specs=in_specs, out_specs=out_specs, check_vma=False
    )
```

```python
import jax
import jax.numpy as jnp
from jax import lax
from jax.experimental import pallas as pl
from jax.experimental.pallas import tpu as pltpu
from jax.sharding import PartitionSpec as P


ITERS = 2
SWEEPS = 3


highest = lax.Precision.HIGHEST
relax_weight = 0.6
f32 = jnp.float32
bf16 = jnp.bfloat16


def matmul(left, right):
    return jnp.dot(left, right, precision=highest, preferred_element_type=jnp.float32)


def distributed(
    probes,
    viscosity,
    friction,
    sensitivity,
    misfit_weight,
    grad_ref,
    trace_ref,
    coarse_modes,
    coarse_inv,
    peer_slots,
    local_pairs,
    elem_agg,
):
    agg_count = lax.axis_size("agg")
    elem_local = viscosity.shape[1]
    slot_flat = peer_slots.reshape(-1)
    filled = slot_flat >= 0
    own_local = jnp.where(filled, slot_flat, 0)
    filled_float = filled.astype(jnp.float32)
    first_end = local_pairs[0]
    second_end = local_pairs[1]
    counts = jnp.zeros((elem_local,), jnp.float32)
    counts = counts.at[first_end].add(1.0).at[second_end].add(1.0).at[own_local].add(filled_float)
    trace_square = jnp.sum(trace_ref * trace_ref, axis=0)
    diag_op = (
        matmul((grad_ref * grad_ref).T, viscosity)
        + friction
        + counts[None, :] * trace_square[:, None]
    )
    group_aggs = agg_count * coarse_inv.shape[0]
    one_hot = (elem_agg[:, None] == jnp.arange(group_aggs, dtype=jnp.int32)[None, :]).astype(
        jnp.float32
    )

    def operate(field_vec):
        inner_term = matmul(grad_ref.T, viscosity * matmul(grad_ref, field_vec))
        traces = matmul(trace_ref, field_vec)
        outgoing = traces[:, own_local] * filled_float[None, :]
        incoming = lax.all_to_all(
            outgoing, ("leaf", "agg"), split_axis=1, concat_axis=1, tiled=True
        )
        cross_diff = outgoing - incoming
        local_diff = traces[:, first_end] - traces[:, second_end]
        accumulated = jnp.zeros_like(field_vec)
        accumulated = (
            accumulated.at[:, first_end].add(local_diff).at[:, second_end].add(-local_diff)
        )
        accumulated = accumulated.at[:, own_local].add(cross_diff)
        return inner_term + friction * field_vec + matmul(trace_ref.T, accumulated)

    def coarse(residual_now):
        projected = matmul(coarse_modes.T, residual_now)
        coarse_sums = matmul(projected, one_hot)
        own_sums = lax.psum_scatter(coarse_sums, "agg", scatter_dimension=1, tiled=True)
        solved_own = jnp.einsum("acd,da->ca", coarse_inv, own_sums, precision=highest)
        solved_all = lax.all_gather(solved_own, "agg", axis=1, tiled=True)
        return matmul(coarse_modes, matmul(solved_all, one_hot.T))

    def precond(residual_now):
        smooth = relax_weight * residual_now / diag_op
        for _ in range(SWEEPS - 1):
            smooth = smooth + relax_weight * (residual_now - operate(smooth)) / diag_op
        return smooth + coarse(residual_now)

    def energy_sum(left, right):
        return lax.psum(jnp.sum(left * right), ("leaf", "agg"))

    def krylov(source):
        residual_now = source
        precon = precond(residual_now)
        search = precon
        energy_now = energy_sum(residual_now, precon)
        iterate = jnp.zeros_like(source)
        for iteration in range(ITERS):
            image_vec = operate(search)
            step_size = energy_now / lax.psum(jnp.sum(search * image_vec), ("leaf", "agg"))
            iterate = iterate + step_size * search
            if iteration + 1 < ITERS:
                residual_now = residual_now - step_size * image_vec
                precon = precond(residual_now)
                energy_next = energy_sum(residual_now, precon)
                search = precon + energy_next / energy_now * search
                energy_now = energy_next
        return iterate

    probe_field = probes[0]
    forward = krylov(sensitivity * probe_field)
    adjoint = krylov(misfit_weight * forward)
    action = sensitivity * adjoint
    trace_value = lax.psum(jnp.sum(probe_field * action), ("leaf", "agg", "probe")) / lax.axis_size(
        "probe"
    )
    return (forward[None], action[None], trace_value)


def split(value):
    high = value.astype(bf16)
    low = (value - high.astype(f32)).astype(bf16)
    return high, low


def dot(left, right):
    return jnp.dot(left, right, preferred_element_type=f32)


def dot_nt(left, right):
    return lax.dot_general(left, right, (((1,), (1,)), ((), ())), preferred_element_type=f32)


def total(value):
    return jnp.sum(jnp.sum(value, axis=0, keepdims=True), axis=1, keepdims=True)


def spec(space):
    return pl.BlockSpec(memory_space=space)


VM = pltpu.VMEM
SM = pltpu.SMEM


def call(kernel, outs, args, spaces=None, scratch=(), flops=0, bytes_accessed=0):
    return kernel_call(kernel, outs, args, spaces, scratch, flops, bytes_accessed)


def kernel_call(kernel, outs, args, spaces, scratch, flops, bytes_accessed):
    spaces = spaces or [VM] * len(args)
    args = [
        pltpu.with_memory_space_constraint(arg, space) if space == pltpu.HBM else arg
        for arg, space in zip(args, spaces)
    ]
    return pl.pallas_call(
        kernel,
        out_shape=[jax.ShapeDtypeStruct(*one) for one in outs],
        in_specs=[spec(space) for space in spaces],
        out_specs=[spec(VM) for _ in outs],
        scratch_shapes=list(scratch),
        compiler_params=pltpu.CompilerParams(vmem_limit_bytes=16 * 1024 * 1024),
        cost_estimate=pl.CostEstimate(
            flops=flops, bytes_accessed=bytes_accessed, transcendentals=0
        ),
    )(*args)


class Dims:
    def __init__(self, ndof, elem, parts, cap, modes, aggs, lines):
        self.ndof, self.elem, self.parts, self.cap = ndof, elem, parts, cap
        self.modes, self.aggs = modes, aggs
        self.lines, self.share = lines, ndof // lines
        self.total = elem * parts
        self.half = parts // 2
        self.group = 2 * aggs
        self.all_aggs = parts * aggs
        self.chunk = 2 * elem


def prepare_constants(dim, grad, trace, modes, g3, gs, gsq3, my, m3t, trsq):
    n = dim.ndof
    high, low = split(grad)
    g3[:, 0:n], g3[:, n : 2 * n], g3[:, 2 * n :] = high, high, low
    gt = grad.T
    tt = trace.T
    gram = lax.dot_general(
        tt, tt, (((1,), (1,)), ((), ())), precision=highest, preferred_element_type=f32
    )
    gh, gl = split(gt)
    sh, sl = split(gram)
    for place, piece in enumerate((gh, sh, gh, sh, gl, sl)):
        gs[:, place * n : (place + 1) * n] = piece
    qh, ql = split(gt * gt)
    gsq3[:, 0:n], gsq3[:, n : 2 * n], gsq3[:, 2 * n :] = qh, qh, ql
    mh, ml = split(modes)
    w = dim.modes
    my[:, 0:w], my[:, w : 2 * w], my[:, 2 * w :] = mh, mh, ml
    th, tl = split(modes.T)
    m3t[:, 0:n], m3t[:, n : 2 * n], m3t[:, 2 * n :] = th, th, tl
    trsq[...] = jnp.sum(tt * tt, axis=1, keepdims=True)


def restrict(field, hot, m3t):
    high, low = split(field)
    sums = dot_nt(high, hot) + dot_nt(low, hot)
    high, low = split(sums)
    return dot(m3t[...], jnp.concatenate([high, low, high], axis=0))


def solve_blocks(sums, first, inv, count):
    rows = []
    for index in range(count):
        column = sums[:, first + index : first + index + 1]
        rows.append(jnp.sum(inv[index] * column, axis=0, keepdims=True))
    return jnp.concatenate(rows, axis=0)


def hot_of(dim, agg_row, agg_index, columns):
    place = lax.broadcasted_iota(jnp.int32, (dim.group, columns), 0)
    wanted = lax.rem(place + agg_index * dim.aggs, dim.group)
    return jnp.where(wanted.astype(f32) == agg_row, 1.0, 0.0).astype(bf16)


def source_kernel(
    dim, place, probe_in, sens_in, pairs_in, slots_in, agg_in, grad_in, trace_in, modes_in, inv_in,
    visc_in, fric_in, weight_in, payload, quarter, sums, g3, gs, gsq3, my, m3t, trsq, inv,
    probe, sens, pairs, slots, agg_row, grad, trace, modes, sems,
):
    moves = (
        (probe_in.at[0], probe),
        (sens_in, sens),
        (pairs_in, pairs),
        (slots_in.at[0], slots),
        (agg_in, agg_row),
        (grad_in, grad),
        (trace_in, trace),
        (modes_in, modes),
        (inv_in, inv),
    )
    share = dim.share
    mine = pl.ds(pl.multiple_of(place[2] * share, share), share)
    moves += tuple(
        (field.at[mine], quarter.at[pl.ds(index * share, share)])
        for index, field in enumerate((visc_in, fric_in, weight_in))
    )
    copies = [
        pltpu.make_async_copy(src, dst, sems.at[index]) for index, (src, dst) in enumerate(moves)
    ]
    for copy in copies:
        copy.start()
    for copy in copies:
        copy.wait()
    n = dim.ndof
    value = probe[...] * sens[...]
    payload[0:n, :] = value
    agg_float = agg_row[...].astype(f32)
    payload[n : n + 2, :] = pairs[...].astype(f32)
    for part in range(dim.parts):
        span = slice(part * dim.cap, (part + 1) * dim.cap)
        payload[n + 2 : n + 3, span] = slots[part : part + 1, :].astype(f32)
    payload[n + 3 : n + 4, :] = agg_float
    payload[n + 4 : n + 8, :] = jnp.zeros((4, dim.elem), f32)
    prepare_constants(dim, grad[...], trace[...], modes[...], g3, gs, gsq3, my, m3t, trsq)
    hot = hot_of(dim, agg_float, 0, dim.elem)
    sums[...] = restrict(value, hot, m3t)


def source_coarse_kernel(
    dim, place, payload, sums_own, sums_partner, inv_own, inv_partner, out
):
    rows = dim.ndof + 8
    agg = place[1]
    out[0:rows, :] = payload[...]
    sums = sums_own[...] + sums_partner[...]
    first, second = sums[:, 0 : dim.aggs], sums[:, dim.aggs :]
    mine = jnp.where(agg == 0, first, second)
    theirs = jnp.where(agg == 0, second, first)
    out[pl.ds(pl.multiple_of(rows + agg * dim.aggs, dim.aggs), dim.aggs), :] = solve_blocks(
        mine, 0, inv_own, dim.aggs
    )
    out[pl.ds(pl.multiple_of(rows + (1 - agg) * dim.aggs, dim.aggs), dim.aggs), :] = solve_blocks(
        theirs, 0, inv_partner, dim.aggs
    )


def stack_kernel(*refs):
    out = refs[-1]
    rows = refs[0].shape[0]
    for index, ref in enumerate(refs[:-1]):
        out[index * rows : (index + 1) * rows, :] = ref[...]


def build_kernel(dim, place, *refs):
    blocks = refs[: dim.parts]
    source, lap, hot2, counts, hot_own, table, sides, agg = refs[dim.parts :]
    n, e = dim.ndof, dim.elem
    for index, ref in enumerate(blocks):
        where = place[4 + index]
        columns = pl.ds(pl.multiple_of(where * e, e), e)
        source[:, columns] = ref[0:n, :]
        sides[pl.ds(where, 1), :] = ref[n : n + 1, :]
        sides[pl.ds(where + dim.parts, 1), :] = ref[n + 1 : n + 2, :]
        table[pl.ds(where, 1), :] = ref[n + 2 : n + 3, :]
        group = (where // 2) * dim.group
        agg[:, columns] = ref[n + 3 : n + 4, :] + group.astype(f32)
    elem_id = lax.broadcasted_iota(jnp.int32, (e, e), 0).astype(f32)
    lane = lax.broadcasted_iota(jnp.int32, (e, e), 1)
    column_id = lax.broadcasted_iota(jnp.int32, (e, e), 1)
    row_id = lax.broadcasted_iota(jnp.int32, (e, e), 0)
    on_diagonal = row_id == column_id
    full = table[...]
    rolled = [full]
    for shift in range(1, dim.parts):
        rolled.append(pltpu.roll(full, shift * dim.cap, 1))
    slot_block = lane // dim.cap
    for p in range(dim.parts):
        mine = jnp.where(full[p : p + 1, :] == elem_id, 1.0, 0.0).astype(bf16)
        first = jnp.where(sides[p : p + 1, :] == elem_id, 1.0, 0.0)
        second = jnp.where(sides[p + dim.parts : p + dim.parts + 1, :] == elem_id, 1.0, 0.0)
        edge = (first - second).astype(bf16)
        local = dot_nt(edge, edge)
        count = jnp.sum(mine.astype(f32), axis=1, keepdims=True)
        for q in range(dim.parts):
            if q == p:
                block = local + jnp.where(on_diagonal, count, 0.0)
                diagonal = jnp.where(on_diagonal, block, 0.0)
                counts[:, p * e : (p + 1) * e] = jnp.sum(diagonal, axis=0, keepdims=True)
            else:
                row = rolled[(q - p) % dim.parts][q : q + 1, :]
                theirs = jnp.where((row == elem_id) & (slot_block == q), 1.0, 0.0).astype(bf16)
                block = -dot_nt(mine, theirs)
            lap[p * e : (p + 1) * e, q * e : (q + 1) * e] = block.astype(bf16)
    agg_id = lax.broadcasted_iota(jnp.int32, (dim.all_aggs, dim.total), 0).astype(f32)
    hot2[...] = jnp.where(agg[...] == agg_id, 1.0, 0.0).astype(bf16)
    leaf = place[0]
    span = 2 * e
    own_row = agg[:, pl.ds(pl.multiple_of(leaf * span, span), span)]
    own_row = own_row - (leaf * dim.group).astype(f32)
    hot_own[...] = hot_of(dim, own_row, place[1], span)


def chunks(dim):
    return [slice(start, start + dim.chunk) for start in range(0, dim.total, dim.chunk)]


def apply_operator(dim, vec, consts, v3, uy, emit):
    visc, fric, lap, g3, gs = consts
    n = dim.ndof
    for c in chunks(dim):
        high, low = split(vec[:, c])
        v3[0:n, c] = high
        v3[n : 2 * n, c] = low
        v3[2 * n : 3 * n, c] = high
    for c in chunks(dim):
        high, low = split(visc[:, c] * dot(g3[...], v3[:, c]))
        uy[0:n, c] = high
        uy[2 * n : 3 * n, c] = low
        uy[4 * n : 5 * n, c] = high
    for c in chunks(dim):
        both = dot(v3[0 : 2 * n, :], lap[:, c])
        high, low = split(both[0:n] + both[n : 2 * n])
        uy[n : 2 * n, c] = high
        uy[3 * n : 4 * n, c] = low
        uy[5 * n : 6 * n, c] = high
    for c in chunks(dim):
        emit(c, dot(gs[...], uy[:, c]) + fric[:, c] * vec[:, c])


def smooth_loop(dim, resid, smooth, w_diag, consts, v3, uy):
    for c in chunks(dim):
        smooth[:, c] = w_diag[:, c] * resid[:, c]

    def sweep(index, carry):
        def emit(c, image):
            smooth[:, c] = smooth[:, c] + w_diag[:, c] * (resid[:, c] - image)

        apply_operator(dim, smooth, consts, v3, uy, emit)
        return carry

    lax.fori_loop(0, SWEEPS - 1, sweep, 0)


def coarse_add(dim, solved, my, hot2, target):
    high, low = split(solved)
    coarse = dot_nt(my[...], jnp.concatenate([high, low, high], axis=1))
    high, low = split(coarse)
    for c in chunks(dim):
        target[:, c] = target[:, c] + dot(high, hot2[:, c]) + dot(low, hot2[:, c])


def group_solve(dim, place, resid, hot_own, m3t, inv_own, inv_partner, out):
    leaf, agg = place[0], place[1]
    span = 2 * dim.elem
    field = resid[:, pl.ds(pl.multiple_of(leaf * span, span), span)]
    sums = restrict(field, hot_own[...], m3t)
    out[pl.ds(pl.multiple_of(agg * dim.aggs, dim.aggs), dim.aggs), :] = solve_blocks(
        sums, 0, inv_own, dim.aggs
    )
    out[pl.ds(pl.multiple_of((1 - agg) * dim.aggs, dim.aggs), dim.aggs), :] = solve_blocks(
        sums, dim.aggs, inv_partner, dim.aggs
    )


def first_step(dim, source, image, consts, v3, uy, resid, search, scal):
    def emit(c, value):
        image[:, c] = value

    apply_operator(dim, search, consts, v3, uy, emit)
    energy = total(source[...] * search[...])
    step = energy / total(search[...] * image[...])
    resid[...] = source[...] - step * image[...]
    scal[0:1, :] = jnp.broadcast_to(energy, (1, 128))
    scal[1:2, :] = jnp.broadcast_to(step, (1, 128))


def second_step(dim, resid, search, precon, scal, consts, v3, uy, image):
    energy = total(resid[...] * precon[...])
    ratio = energy / scal[0:1, 0:1]
    precon[...] = precon[...] + ratio * search[...]

    def emit(c, value):
        image[:, c] = value

    apply_operator(dim, precon, consts, v3, uy, emit)
    step = energy / total(precon[...] * image[...])
    precon[...] = scal[1:2, 0:1] * search[...] + step * precon[...]


def gather_parts(dim, place, parts, solved):
    groups = []
    for ref in parts:
        first = dim.ndof + 8 if ref.shape[0] > dim.ndof else 0
        groups += [(ref, step) for step in range(first, ref.shape[0], dim.group)]
    for index, (ref, first) in enumerate(groups):
        where = place[4 + index] // 2
        solved[pl.ds(pl.multiple_of(where * dim.group, dim.group), dim.group), :] = ref[
            first : first + dim.group, :
        ]


def begin_kernel(dim, place, source, counts, trsq, lap, g3, gs, gsq3, *refs):
    e = dim.elem
    stacks = refs[: 2 * dim.lines]
    visc, fric, weight, w_diag, smooth, v3, uy = refs[2 * dim.lines :]
    share = dim.share
    for index, ref in enumerate(stacks):
        line = place[2] ^ (index % dim.lines)
        rows = pl.ds(pl.multiple_of(line * share, share), share)
        for chip in range(dim.half):
            where = place[4 + chip + dim.half * (index // dim.lines)]
            columns = pl.ds(pl.multiple_of(where * e, e), e)
            for number, field in enumerate((visc, fric, weight)):
                start = (3 * chip + number) * share
                field[rows, columns] = ref[start : start + share, :]
    for c in chunks(dim):
        high, low = split(visc[:, c])
        diag = dot(gsq3[...], jnp.concatenate([high, low, high], axis=0))
        diag = diag + fric[:, c] + counts[:, c] * trsq[...]
        w_diag[:, c] = relax_weight / diag
    smooth_loop(dim, source, smooth, w_diag, (visc, fric, lap, g3, gs), v3, uy)


def sweep_kernel(dim, first, resid, visc, fric, w_diag, lap, g3, gs, *refs):
    if first:
        smooth, v3, uy, start = refs
        for c in chunks(dim):
            start[:, c] = w_diag[:, c] * resid[:, c]
    else:
        start, smooth, v3, uy = refs

    def emit(c, image):
        smooth[:, c] = start[:, c] + w_diag[:, c] * (resid[:, c] - image)

    apply_operator(dim, start, (visc, fric, lap, g3, gs), v3, uy, emit)


def middle_kernel(
    dim, place, smooth, resid, search, scal, weight, visc, fric, lap, g3, gs, hot2, my, m3t,
    hot_own, inv_own, inv_partner, *refs,
):
    parts = refs[:-8]
    iterate, source, out, v3, uy, image, solved, precon = refs[-8:]
    e = dim.elem
    gather_parts(dim, place, parts, solved)
    precon[...] = smooth[...]
    coarse_add(dim, solved[...], my, hot2, precon)
    consts = (visc, fric, lap, g3, gs)
    second_step(dim, resid, search, precon, scal, consts, v3, uy, image)
    mine = pl.ds(pl.multiple_of(place[4] * e, e), e)
    iterate[...] = precon[:, mine]
    source[...] = weight[...] * precon[...]
    group_solve(dim, place, source, hot_own, m3t, inv_own, inv_partner, out)


def step_kernel(
    dim, place, smooth, source, visc, fric, lap, g3, gs, hot2, my, m3t, hot_own, inv_own,
    inv_partner, *refs,
):
    parts = refs[:-8]
    search, resid, scal, out, v3, uy, image, solved = refs[-8:]
    gather_parts(dim, place, parts, solved)
    search[...] = smooth[...]
    coarse_add(dim, solved[...], my, hot2, search)
    consts = (visc, fric, lap, g3, gs)
    first_step(dim, source, image, consts, v3, uy, resid, search, scal)
    group_solve(dim, place, resid, hot_own, m3t, inv_own, inv_partner, out)


def final_kernel(
    dim, place, smooth, resid, search, scal, source, sens, visc, fric, lap, g3, gs, hot2, my, *refs
):
    parts = refs[:-7]
    action, trace, v3, uy, image, solved, precon = refs[-7:]
    e = dim.elem
    gather_parts(dim, place, parts, solved)
    precon[...] = smooth[...]
    coarse_add(dim, solved[...], my, hot2, precon)
    consts = (visc, fric, lap, g3, gs)
    second_step(dim, resid, search, precon, scal, consts, v3, uy, image)
    mine = pl.ds(pl.multiple_of(place[4] * e, e), e)
    action[...] = sens[...] * precon[:, mine]
    trace[...] = jnp.broadcast_to(total(source[...] * precon[...]), (1, 128))


def replicated(
    probes,
    viscosity,
    friction,
    sensitivity,
    misfit_weight,
    grad_ref,
    trace_ref,
    coarse_modes,
    coarse_inv,
    peer_slots,
    local_pairs,
    elem_agg,
):
    leaf_count = lax.axis_size("leaf")
    dim = Dims(
        viscosity.shape[0],
        viscosity.shape[1],
        2 * leaf_count,
        peer_slots.shape[2],
        coarse_modes.shape[1],
        coarse_inv.shape[0],
        lax.axis_size("probe"),
    )
    n, e, ne = dim.ndof, dim.elem, dim.total
    leaf, agg = lax.axis_index("leaf"), lax.axis_index("agg")
    order = jnp.arange(dim.half, dtype=jnp.int32)
    chips = leaf ^ order
    place = jnp.concatenate(
        [
            jnp.stack([leaf, agg, lax.axis_index("probe"), leaf]),
            chips * 2 + agg,
            chips * 2 + (1 - agg),
        ]
    ).astype(jnp.int32)
    flip = [(0, 1), (1, 0)]

    def to_partner(value):
        return lax.ppermute(value, "agg", flip)

    def peers(value):
        found = [value]
        for step in range(1, leaf_count):
            pairs = [(index, index ^ step) for index in range(leaf_count)]
            found.append(lax.ppermute(value, "leaf", pairs))
        return found

    def gather(value):
        own = peers(value)
        return own + [to_partner(one) for one in own]

    payload, quarter, sums, g3, gs, gsq3, my, m3t, trsq, inv_own = call(
        lambda *refs: source_kernel(dim, *refs),
        [
            ((n + 8, e), f32),
            ((3 * dim.share, e), f32),
            ((dim.modes, dim.group), f32),
            ((n, 3 * n), bf16),
            ((n, 6 * n), bf16),
            ((n, 3 * n), bf16),
            ((n, 3 * dim.modes), bf16),
            ((dim.modes, 3 * n), bf16),
            ((n, 1), f32),
            (coarse_inv.shape, f32),
        ],
        [place, probes, sensitivity, local_pairs, peer_slots, elem_agg.reshape(1, e)]
        + [grad_ref, trace_ref, coarse_modes, coarse_inv, viscosity, friction, misfit_weight],
        [SM] + [pltpu.HBM] * 12,
        scratch=[
            VM((n, e), f32),
            VM((n, e), f32),
            VM((2, e), jnp.int32),
            VM((dim.parts, dim.cap), jnp.int32),
            VM((1, e), jnp.int32),
            VM((n, n), f32),
            VM((n, n), f32),
            VM((n, dim.modes), f32),
            pltpu.SemaphoreType.DMA((12,)),
        ],
        flops=10**8,
    )
    (stack,) = call(stack_kernel, [((3 * dim.share * dim.half, e), f32)], peers(quarter))
    stacks = [stack]
    for step in range(1, dim.lines):
        pairs = [(index, index ^ step) for index in range(dim.lines)]
        stacks.append(lax.ppermute(stack, "probe", pairs))
    stacks += [to_partner(one) for one in stacks]
    inv_partner = to_partner(inv_own)
    sums_partner = to_partner(sums)
    (payload,) = call(
        lambda *refs: source_coarse_kernel(dim, *refs),
        [((n + 8 + dim.group, e), f32)],
        [place, payload, sums, sums_partner, inv_own, inv_partner],
        [SM, VM, VM, VM, VM, VM],
    )
    source_blocks = gather(payload)
    parts = source_blocks[: dim.half]

    field = ((n, ne), f32)
    source, lap, hot2, counts, hot_own = call(
        lambda *refs: build_kernel(dim, *refs),
        [
            field,
            ((ne, ne), bf16),
            ((dim.all_aggs, ne), bf16),
            ((1, ne), f32),
            ((dim.group, 2 * e), bf16),
        ],
        [place] + source_blocks,
        [SM] + [VM] * dim.parts,
        scratch=[VM((dim.parts, e), f32), VM((2 * dim.parts, e), f32), VM((1, ne), f32)],
    )
    work = [VM((3 * n, ne), bf16), VM((6 * n, ne), bf16)]
    image = VM((n, ne), f32)
    solved = VM((dim.all_aggs, dim.modes), f32)
    scal_shape = ((8, 128), f32)
    out_shape = ((dim.group, dim.modes), f32)
    once = 2 * ne * n * (9 * n + 2 * ne)

    visc, fric, weight, w_diag, smooth = call(
        lambda *refs: begin_kernel(dim, *refs),
        [field] * 5,
        [place, source, counts, trsq, lap, g3, gs, gsq3] + stacks,
        [SM] + [VM] * (7 + len(stacks)),
        scratch=work,
        flops=2 * once,
    )

    def sweep_of(first, args):
        (found,) = call(
            lambda *refs: sweep_kernel(dim, first, *refs),
            [field],
            args,
            scratch=work + ([image] if first else []),
            flops=once,
        )
        return found

    def smooth_and_spread(value, solved_group):
        consts = [value, visc, fric, w_diag, lap, g3, gs]
        smooth, found = None, solved_group
        parts = [solved_group]
        for sweep in range(SWEEPS - 1):
            width = 2**sweep
            if width < leaf_count:
                pairs = [(index, index ^ width) for index in range(leaf_count)]
                other = lax.ppermute(found, "leaf", pairs)
                parts.append(other)
                if 2 * width < leaf_count:
                    found = jnp.concatenate([found, other], axis=0)
            smooth = sweep_of(sweep == 0, consts if sweep == 0 else consts + [smooth])
        return smooth, parts

    def step_of(smooth, start, parts):
        return call(
            lambda *refs: step_kernel(dim, *refs),
            [field, field, scal_shape, out_shape],
            [place, smooth, start, visc, fric, lap, g3, gs, hot2, my, m3t, hot_own, inv_own]
            + [inv_partner]
            + parts,
            [SM] + [VM] * (13 + len(parts)),
            scratch=work + [image, solved],
            flops=once,
        )

    search, resid, scal, out = step_of(smooth, source, parts)
    smooth, parts = smooth_and_spread(resid, out)
    iterate, source_two, out = call(
        lambda *refs: middle_kernel(dim, *refs),
        [((n, e), f32), field, out_shape],
        [place, smooth, resid, search, scal, weight, visc, fric, lap, g3, gs, hot2, my]
        + [m3t, hot_own, inv_own, inv_partner]
        + parts,
        [SM] + [VM] * (16 + len(parts)),
        scratch=work + [image, solved, image],
        flops=once,
    )
    smooth, parts = smooth_and_spread(source_two, out)
    search, resid, scal, out = step_of(smooth, source_two, parts)
    smooth, parts = smooth_and_spread(resid, out)
    action, trace = call(
        lambda *refs: final_kernel(dim, *refs),
        [((n, e), f32), ((1, 128), f32)],
        [place, smooth, resid, search, scal, source, sensitivity, visc, fric, lap, g3, gs, hot2]
        + [my]
        + parts,
        [SM] + [VM] * (13 + len(parts)),
        scratch=work + [image, solved, image],
        flops=once,
    )
    probe_count = lax.axis_size("probe")
    traces = [trace]
    for step in range(1, probe_count):
        pairs = [(index, (index + step) % probe_count) for index in range(probe_count)]
        if probe_count & (probe_count - 1) == 0:
            pairs = [(index, index ^ step) for index in range(probe_count)]
        traces.append(lax.ppermute(trace, "probe", pairs))
    trace_value = sum(one[0, 0] for one in traces) / probe_count
    return iterate[None], action[None], trace_value


def fits_one_core(mesh, viscosity, coarse_modes, coarse_inv, peer_slots, local_pairs):
    leaf_count, agg_count, probe_count = (mesh.shape[name] for name in ("leaf", "agg", "probe"))
    ndof, elem = viscosity.shape
    parts = leaf_count * agg_count
    cap = peer_slots.shape[2]
    aggs = coarse_inv.shape[0]
    return (
        agg_count == 2
        and leaf_count & (leaf_count - 1) == 0
        and leaf_count <= 2 ** (SWEEPS - 1)
        and elem == 128
        and coarse_modes.shape[1] == 128
        and parts * cap == elem
        and local_pairs.shape[1] == elem
        and ndof % 16 == 0
        and ndof % (8 * probe_count) == 0
        and probe_count & (probe_count - 1) == 0
        and aggs % 8 == 0
        and local_pairs.shape[1] + (parts - 1) * cap <= 256
        and parts * elem <= 1024
    )


def solution(mesh):
    in_specs = (
        P("probe", None, ("leaf", "agg")),
        P(None, ("leaf", "agg")),
        P(None, ("leaf", "agg")),
        P(None, ("leaf", "agg")),
        P(None, ("leaf", "agg")),
        P(),
        P(),
        P(),
        P(("leaf", "agg"), None, None),
        P(("leaf", "agg"), None, None),
        P(None, ("leaf", "agg")),
        P(("leaf", "agg")),
    )
    out_specs = (P("probe", None, ("leaf", "agg")), P("probe", None, ("leaf", "agg")), P())

    def on_device(*args):
        if fits_one_core(mesh, args[1], args[7], args[8], args[9], args[10]):
            return replicated(*args)
        return distributed(*args)

    return jax.shard_map(
        on_device, mesh=mesh, in_specs=in_specs, out_specs=out_specs, check_vma=False
    )
```

```python
import jax
import jax.numpy as jnp
from jax import lax
from jax.experimental import pallas as pl
from jax.experimental.pallas import tpu as pltpu
from jax.sharding import PartitionSpec as P


ITERS = 2
SWEEPS = 3


highest = lax.Precision.HIGHEST
relax_weight = 0.6
f32 = jnp.float32
bf16 = jnp.bfloat16


def matmul(left, right):
    return jnp.dot(left, right, precision=highest, preferred_element_type=jnp.float32)


def distributed(
    probes,
    viscosity,
    friction,
    sensitivity,
    misfit_weight,
    grad_ref,
    trace_ref,
    coarse_modes,
    coarse_inv,
    peer_slots,
    local_pairs,
    elem_agg,
):
    agg_count = lax.axis_size("agg")
    elem_local = viscosity.shape[1]
    slot_flat = peer_slots.reshape(-1)
    filled = slot_flat >= 0
    own_local = jnp.where(filled, slot_flat, 0)
    filled_float = filled.astype(jnp.float32)
    first_end = local_pairs[0]
    second_end = local_pairs[1]
    counts = jnp.zeros((elem_local,), jnp.float32)
    counts = counts.at[first_end].add(1.0).at[second_end].add(1.0).at[own_local].add(filled_float)
    trace_square = jnp.sum(trace_ref * trace_ref, axis=0)
    diag_op = (
        matmul((grad_ref * grad_ref).T, viscosity)
        + friction
        + counts[None, :] * trace_square[:, None]
    )
    group_aggs = agg_count * coarse_inv.shape[0]
    one_hot = (elem_agg[:, None] == jnp.arange(group_aggs, dtype=jnp.int32)[None, :]).astype(
        jnp.float32
    )

    def operate(field_vec):
        inner_term = matmul(grad_ref.T, viscosity * matmul(grad_ref, field_vec))
        traces = matmul(trace_ref, field_vec)
        outgoing = traces[:, own_local] * filled_float[None, :]
        incoming = lax.all_to_all(
            outgoing, ("leaf", "agg"), split_axis=1, concat_axis=1, tiled=True
        )
        cross_diff = outgoing - incoming
        local_diff = traces[:, first_end] - traces[:, second_end]
        accumulated = jnp.zeros_like(field_vec)
        accumulated = (
            accumulated.at[:, first_end].add(local_diff).at[:, second_end].add(-local_diff)
        )
        accumulated = accumulated.at[:, own_local].add(cross_diff)
        return inner_term + friction * field_vec + matmul(trace_ref.T, accumulated)

    def coarse(residual_now):
        projected = matmul(coarse_modes.T, residual_now)
        coarse_sums = matmul(projected, one_hot)
        own_sums = lax.psum_scatter(coarse_sums, "agg", scatter_dimension=1, tiled=True)
        solved_own = jnp.einsum("acd,da->ca", coarse_inv, own_sums, precision=highest)
        solved_all = lax.all_gather(solved_own, "agg", axis=1, tiled=True)
        return matmul(coarse_modes, matmul(solved_all, one_hot.T))

    def precond(residual_now):
        smooth = relax_weight * residual_now / diag_op
        for _ in range(SWEEPS - 1):
            smooth = smooth + relax_weight * (residual_now - operate(smooth)) / diag_op
        return smooth + coarse(residual_now)

    def energy_sum(left, right):
        return lax.psum(jnp.sum(left * right), ("leaf", "agg"))

    def krylov(source):
        residual_now = source
        precon = precond(residual_now)
        search = precon
        energy_now = energy_sum(residual_now, precon)
        iterate = jnp.zeros_like(source)
        for iteration in range(ITERS):
            image_vec = operate(search)
            step_size = energy_now / lax.psum(jnp.sum(search * image_vec), ("leaf", "agg"))
            iterate = iterate + step_size * search
            if iteration + 1 < ITERS:
                residual_now = residual_now - step_size * image_vec
                precon = precond(residual_now)
                energy_next = energy_sum(residual_now, precon)
                search = precon + energy_next / energy_now * search
                energy_now = energy_next
        return iterate

    probe_field = probes[0]
    forward = krylov(sensitivity * probe_field)
    adjoint = krylov(misfit_weight * forward)
    action = sensitivity * adjoint
    trace_value = lax.psum(jnp.sum(probe_field * action), ("leaf", "agg", "probe")) / lax.axis_size(
        "probe"
    )
    return (forward[None], action[None], trace_value)


def split(value):
    high = value.astype(bf16)
    low = (value - high.astype(f32)).astype(bf16)
    return high, low


def dot(left, right):
    return jnp.dot(left, right, preferred_element_type=f32)


def dot_nt(left, right):
    return lax.dot_general(left, right, (((1,), (1,)), ((), ())), preferred_element_type=f32)


def total(value):
    return jnp.sum(jnp.sum(value, axis=0, keepdims=True), axis=1, keepdims=True)


def spec(space):
    return pl.BlockSpec(memory_space=space)


VM = pltpu.VMEM
SM = pltpu.SMEM


def call(kernel, outs, args, spaces=None, scratch=(), flops=0, bytes_accessed=0):
    return kernel_call(kernel, outs, args, spaces, scratch, flops, bytes_accessed)


def kernel_call(kernel, outs, args, spaces, scratch, flops, bytes_accessed):
    spaces = spaces or [VM] * len(args)
    args = [
        pltpu.with_memory_space_constraint(arg, space) if space == pltpu.HBM else arg
        for arg, space in zip(args, spaces)
    ]
    return pl.pallas_call(
        kernel,
        out_shape=[jax.ShapeDtypeStruct(*one) for one in outs],
        in_specs=[spec(space) for space in spaces],
        out_specs=[spec(VM) for _ in outs],
        scratch_shapes=list(scratch),
        compiler_params=pltpu.CompilerParams(vmem_limit_bytes=16 * 1024 * 1024),
        cost_estimate=pl.CostEstimate(
            flops=flops, bytes_accessed=bytes_accessed, transcendentals=0
        ),
    )(*args)


class Dims:
    def __init__(self, ndof, elem, parts, cap, modes, aggs, lines):
        self.ndof, self.elem, self.parts, self.cap = ndof, elem, parts, cap
        self.modes, self.aggs = modes, aggs
        self.lines, self.share = lines, ndof // lines
        self.total = elem * parts
        self.half = parts // 2
        self.group = 2 * aggs
        self.all_aggs = parts * aggs
        self.chunk = 2 * elem


def prepare_constants(dim, grad, trace, modes, g3, gs, gsq3, my, m3t, trsq):
    n = dim.ndof
    high, low = split(grad)
    g3[:, 0:n], g3[:, n : 2 * n], g3[:, 2 * n :] = high, high, low
    gt = grad.T
    tt = trace.T
    gram = lax.dot_general(
        tt, tt, (((1,), (1,)), ((), ())), precision=highest, preferred_element_type=f32
    )
    gh, gl = split(gt)
    sh, sl = split(gram)
    for place, piece in enumerate((gh, sh, gh, sh, gl, sl)):
        gs[:, place * n : (place + 1) * n] = piece
    qh, ql = split(gt * gt)
    gsq3[:, 0:n], gsq3[:, n : 2 * n], gsq3[:, 2 * n :] = qh, qh, ql
    mh, ml = split(modes)
    w = dim.modes
    my[:, 0:w], my[:, w : 2 * w], my[:, 2 * w :] = mh, mh, ml
    th, tl = split(modes.T)
    m3t[:, 0:n], m3t[:, n : 2 * n], m3t[:, 2 * n :] = th, th, tl
    trsq[...] = jnp.sum(tt * tt, axis=1, keepdims=True)


def restrict(field, hot, m3t):
    high, low = split(field)
    sums = dot_nt(high, hot) + dot_nt(low, hot)
    high, low = split(sums)
    return dot(m3t[...], jnp.concatenate([high, low, high], axis=0))


def solve_blocks(sums, first, inv, count):
    rows = []
    for index in range(count):
        column = sums[:, first + index : first + index + 1]
        rows.append(jnp.sum(inv[index] * column, axis=0, keepdims=True))
    return jnp.concatenate(rows, axis=0)


def hot_of(dim, agg_row, agg_index, columns):
    place = lax.broadcasted_iota(jnp.int32, (dim.group, columns), 0)
    wanted = lax.rem(place + agg_index * dim.aggs, dim.group)
    return jnp.where(wanted.astype(f32) == agg_row, 1.0, 0.0).astype(bf16)


def source_kernel(
    dim, place, probe_in, sens_in, pairs_in, slots_in, agg_in, grad_in, trace_in, modes_in, inv_in,
    visc_in, fric_in, weight_in, payload, quarter, sums, g3, gs, gsq3, my, m3t, trsq, inv,
    probe, sens, pairs, slots, agg_row, grad, trace, modes, sems,
):
    moves = (
        (probe_in.at[0], probe),
        (sens_in, sens),
        (pairs_in, pairs),
        (slots_in.at[0], slots),
        (agg_in, agg_row),
        (grad_in, grad),
        (trace_in, trace),
        (modes_in, modes),
        (inv_in, inv),
    )
    share = dim.share
    mine = pl.ds(pl.multiple_of(place[2] * share, share), share)
    moves += tuple(
        (field.at[mine], quarter.at[pl.ds(index * share, share)])
        for index, field in enumerate((visc_in, fric_in, weight_in))
    )
    copies = [
        pltpu.make_async_copy(src, dst, sems.at[index]) for index, (src, dst) in enumerate(moves)
    ]
    for copy in copies:
        copy.start()
    for copy in copies:
        copy.wait()
    n = dim.ndof
    value = probe[...] * sens[...]
    payload[0:n, :] = value
    agg_float = agg_row[...].astype(f32)
    payload[n : n + 2, :] = pairs[...].astype(f32)
    for part in range(dim.parts):
        span = slice(part * dim.cap, (part + 1) * dim.cap)
        payload[n + 2 : n + 3, span] = slots[part : part + 1, :].astype(f32)
    payload[n + 3 : n + 4, :] = agg_float
    payload[n + 4 : n + 8, :] = jnp.zeros((4, dim.elem), f32)
    prepare_constants(dim, grad[...], trace[...], modes[...], g3, gs, gsq3, my, m3t, trsq)
    hot = hot_of(dim, agg_float, 0, dim.elem)
    sums[...] = restrict(value, hot, m3t)


def source_coarse_kernel(
    dim, place, payload, sums_own, sums_partner, inv_own, inv_partner, out
):
    rows = dim.ndof + 8
    agg = place[1]
    out[0:rows, :] = payload[...]
    sums = sums_own[...] + sums_partner[...]
    first, second = sums[:, 0 : dim.aggs], sums[:, dim.aggs :]
    mine = jnp.where(agg == 0, first, second)
    theirs = jnp.where(agg == 0, second, first)
    out[pl.ds(pl.multiple_of(rows + agg * dim.aggs, dim.aggs), dim.aggs), :] = solve_blocks(
        mine, 0, inv_own, dim.aggs
    )
    out[pl.ds(pl.multiple_of(rows + (1 - agg) * dim.aggs, dim.aggs), dim.aggs), :] = solve_blocks(
        theirs, 0, inv_partner, dim.aggs
    )


def stack_kernel(*refs):
    out = refs[-1]
    rows = refs[0].shape[0]
    for index, ref in enumerate(refs[:-1]):
        out[index * rows : (index + 1) * rows, :] = ref[...]


def build_kernel(dim, place, *refs):
    blocks = refs[: dim.parts]
    source, lap, hot2, counts, hot_own, table, sides, agg = refs[dim.parts :]
    n, e = dim.ndof, dim.elem
    for index, ref in enumerate(blocks):
        where = place[4 + index]
        columns = pl.ds(pl.multiple_of(where * e, e), e)
        source[:, columns] = ref[0:n, :]
        sides[pl.ds(where, 1), :] = ref[n : n + 1, :]
        sides[pl.ds(where + dim.parts, 1), :] = ref[n + 1 : n + 2, :]
        table[pl.ds(where, 1), :] = ref[n + 2 : n + 3, :]
        group = (where // 2) * dim.group
        agg[:, columns] = ref[n + 3 : n + 4, :] + group.astype(f32)
    elem_id = lax.broadcasted_iota(jnp.int32, (e, e), 0).astype(f32)
    lane = lax.broadcasted_iota(jnp.int32, (e, e), 1)
    column_id = lax.broadcasted_iota(jnp.int32, (e, e), 1)
    row_id = lax.broadcasted_iota(jnp.int32, (e, e), 0)
    on_diagonal = row_id == column_id
    full = table[...]
    rolled = [full]
    for shift in range(1, dim.parts):
        rolled.append(pltpu.roll(full, shift * dim.cap, 1))
    slot_block = lane // dim.cap
    for p in range(dim.parts):
        mine = jnp.where(full[p : p + 1, :] == elem_id, 1.0, 0.0).astype(bf16)
        first = jnp.where(sides[p : p + 1, :] == elem_id, 1.0, 0.0)
        second = jnp.where(sides[p + dim.parts : p + dim.parts + 1, :] == elem_id, 1.0, 0.0)
        edge = (first - second).astype(bf16)
        local = dot_nt(edge, edge)
        count = jnp.sum(mine.astype(f32), axis=1, keepdims=True)
        for q in range(dim.parts):
            if q == p:
                block = local + jnp.where(on_diagonal, count, 0.0)
                diagonal = jnp.where(on_diagonal, block, 0.0)
                counts[:, p * e : (p + 1) * e] = jnp.sum(diagonal, axis=0, keepdims=True)
            else:
                row = rolled[(q - p) % dim.parts][q : q + 1, :]
                theirs = jnp.where((row == elem_id) & (slot_block == q), 1.0, 0.0).astype(bf16)
                block = -dot_nt(mine, theirs)
            lap[p * e : (p + 1) * e, q * e : (q + 1) * e] = block.astype(bf16)
    agg_id = lax.broadcasted_iota(jnp.int32, (dim.all_aggs, dim.total), 0).astype(f32)
    hot2[...] = jnp.where(agg[...] == agg_id, 1.0, 0.0).astype(bf16)
    leaf = place[0]
    span = 2 * e
    own_row = agg[:, pl.ds(pl.multiple_of(leaf * span, span), span)]
    own_row = own_row - (leaf * dim.group).astype(f32)
    hot_own[...] = hot_of(dim, own_row, place[1], span)


def chunks(dim):
    return [slice(start, start + dim.chunk) for start in range(0, dim.total, dim.chunk)]


def apply_operator(dim, vec, consts, v3, uy, emit):
    visc, fric, lap, g3, gs = consts
    n = dim.ndof
    for c in chunks(dim):
        high, low = split(vec[:, c])
        v3[0:n, c] = high
        v3[n : 2 * n, c] = low
        v3[2 * n : 3 * n, c] = high
    for c in chunks(dim):
        high, low = split(visc[:, c] * dot(g3[...], v3[:, c]))
        uy[0:n, c] = high
        uy[2 * n : 3 * n, c] = low
        uy[4 * n : 5 * n, c] = high
    for c in chunks(dim):
        both = dot(v3[0 : 2 * n, :], lap[:, c])
        high, low = split(both[0:n] + both[n : 2 * n])
        uy[n : 2 * n, c] = high
        uy[3 * n : 4 * n, c] = low
        uy[5 * n : 6 * n, c] = high
    for c in chunks(dim):
        emit(c, dot(gs[...], uy[:, c]) + fric[:, c] * vec[:, c])


def smooth_loop(dim, resid, smooth, w_diag, consts, v3, uy):
    for c in chunks(dim):
        smooth[:, c] = w_diag[:, c] * resid[:, c]

    def sweep(index, carry):
        def emit(c, image):
            smooth[:, c] = smooth[:, c] + w_diag[:, c] * (resid[:, c] - image)

        apply_operator(dim, smooth, consts, v3, uy, emit)
        return carry

    lax.fori_loop(0, SWEEPS - 1, sweep, 0)


def coarse_add(dim, solved, my, hot2, base, target):
    high, low = split(solved)
    coarse = dot_nt(my[...], jnp.concatenate([high, low, high], axis=1))
    high, low = split(coarse)
    for c in chunks(dim):
        target[:, c] = base[:, c] + (dot(high, hot2[:, c]) + dot(low, hot2[:, c]))


def group_columns(dim, place):
    span = 2 * dim.elem
    return pl.ds(pl.multiple_of(place[0] * span, span), span)


def group_solve(dim, place, field, hot_own, m3t, inv_own, inv_partner, out, first):
    agg = place[1]
    sums = restrict(field, hot_own[...], m3t)
    out[pl.ds(pl.multiple_of(first + agg * dim.aggs, dim.aggs), dim.aggs), :] = solve_blocks(
        sums, 0, inv_own, dim.aggs
    )
    out[pl.ds(pl.multiple_of(first + (1 - agg) * dim.aggs, dim.aggs), dim.aggs), :] = solve_blocks(
        sums, dim.aggs, inv_partner, dim.aggs
    )


def inner(dim, left, right):
    return total(sum(left[:, c] * right[:, c] for c in chunks(dim)))


def gather_parts(dim, place, parts, tables):
    width = dim.group * len(tables)
    groups = []
    for ref in parts:
        first = dim.ndof + 8 if ref.shape[0] > dim.ndof else 0
        groups += [(ref, step) for step in range(first, ref.shape[0], width)]
    for index, (ref, first) in enumerate(groups):
        where = place[4 + index] // 2
        rows = pl.ds(pl.multiple_of(where * dim.group, dim.group), dim.group)
        for number, table in enumerate(tables):
            start = first + number * dim.group
            table[rows, :] = ref[start : start + dim.group, :]


def begin_kernel(dim, place, source, counts, trsq, lap, g3, gs, gsq3, *refs):
    e = dim.elem
    stacks = refs[: 2 * dim.lines]
    visc, fric, weight, w_diag, smooth, v3, uy = refs[2 * dim.lines :]
    share = dim.share
    for index, ref in enumerate(stacks):
        line = place[2] ^ (index % dim.lines)
        rows = pl.ds(pl.multiple_of(line * share, share), share)
        for chip in range(dim.half):
            where = place[4 + chip + dim.half * (index // dim.lines)]
            columns = pl.ds(pl.multiple_of(where * e, e), e)
            for number, field in enumerate((visc, fric, weight)):
                start = (3 * chip + number) * share
                field[rows, columns] = ref[start : start + share, :]
    for c in chunks(dim):
        high, low = split(visc[:, c])
        diag = dot(gsq3[...], jnp.concatenate([high, low, high], axis=0))
        diag = diag + fric[:, c] + counts[:, c] * trsq[...]
        w_diag[:, c] = relax_weight / diag
    smooth_loop(dim, source, smooth, w_diag, (visc, fric, lap, g3, gs), v3, uy)


def sweep_kernel(dim, first, resid, visc, fric, w_diag, lap, g3, gs, *refs):
    if first:
        smooth, v3, uy, start = refs
        for c in chunks(dim):
            start[:, c] = w_diag[:, c] * resid[:, c]
    else:
        start, smooth, v3, uy = refs

    def emit(c, image):
        smooth[:, c] = start[:, c] + w_diag[:, c] * (resid[:, c] - image)

    apply_operator(dim, start, (visc, fric, lap, g3, gs), v3, uy, emit)


def residual_kernel(
    dim, source, search, image, visc, fric, w_diag, lap, g3, gs, smooth, resid, scal, v3, uy, start
):
    energy = inner(dim, source, search)
    step = energy / inner(dim, search, image)
    scal[0:1, :] = jnp.broadcast_to(energy, (1, 128))
    scal[1:2, :] = jnp.broadcast_to(step, (1, 128))
    for c in chunks(dim):
        value = source[:, c] - step * image[:, c]
        resid[:, c] = value
        start[:, c] = w_diag[:, c] * value

    def emit(c, image_part):
        smooth[:, c] = start[:, c] + w_diag[:, c] * (resid[:, c] - image_part)

    apply_operator(dim, start, (visc, fric, lap, g3, gs), v3, uy, emit)


def step_kernel(
    dim, place, smooth, visc, fric, lap, g3, gs, hot2, my, m3t, hot_own, inv_own,
    inv_partner, *refs,
):
    parts = refs[:-6]
    search, image, out, solved, v3, uy = refs[-6:]
    gather_parts(dim, place, parts, [solved])
    coarse_add(dim, solved[...], my, hot2, smooth, search)

    def emit(c, value):
        image[:, c] = value

    apply_operator(dim, search, (visc, fric, lap, g3, gs), v3, uy, emit)
    field = image[:, group_columns(dim, place)]
    group_solve(dim, place, field, hot_own, m3t, inv_own, inv_partner, out, 0)


def turn(dim, place, parts, smooth, resid, search, scal, solved, my, hot2, table, direction):
    gather_parts(dim, place, parts, [table])
    now = solved[...] - scal[1:2, 0:1] * table[...]
    coarse_add(dim, now, my, hot2, smooth, direction)
    energy = inner(dim, resid, direction)
    ratio = energy / scal[0:1, 0:1]
    for c in chunks(dim):
        direction[:, c] = direction[:, c] + ratio * search[:, c]
    return energy


def last_step(dim, energy, direction, consts, v3, uy):
    sums = []

    def emit(c, value):
        sums.append(jnp.sum(direction[:, c] * value, axis=0, keepdims=True))

    apply_operator(dim, direction, consts, v3, uy, emit)
    return energy / total(sum(sums))


def middle_kernel(
    dim, place, smooth, resid, search, scal, solved, weight, visc, fric, lap, g3, gs, hot2, my,
    m3t, hot_own, inv_own, inv_partner, *refs,
):
    parts = refs[:-7]
    iterate, source, out, v3, uy, table, direction = refs[-7:]
    energy = turn(
        dim, place, parts, smooth, resid, search, scal, solved, my, hot2, table, direction
    )
    step = last_step(dim, energy, direction, (visc, fric, lap, g3, gs), v3, uy)
    first = scal[1:2, 0:1]
    for c in chunks(dim):
        source[:, c] = weight[:, c] * (first * search[:, c] + step * direction[:, c])
    mine = pl.ds(pl.multiple_of(place[4] * dim.elem, dim.elem), dim.elem)
    iterate[...] = first * search[:, mine] + step * direction[:, mine]
    field = source[:, group_columns(dim, place)]
    group_solve(dim, place, field, hot_own, m3t, inv_own, inv_partner, out, 0)


def final_kernel(
    dim, place, smooth, resid, search, scal, solved, source, sens, visc, fric, lap, g3, gs, hot2,
    my, *refs,
):
    parts = refs[:-6]
    action, trace, v3, uy, table, direction = refs[-6:]
    energy = turn(
        dim, place, parts, smooth, resid, search, scal, solved, my, hot2, table, direction
    )
    with_search = inner(dim, source, search)
    with_direction = inner(dim, source, direction)
    step = last_step(dim, energy, direction, (visc, fric, lap, g3, gs), v3, uy)
    first = scal[1:2, 0:1]
    mine = pl.ds(pl.multiple_of(place[4] * dim.elem, dim.elem), dim.elem)
    trace[...] = jnp.broadcast_to(first * with_search + step * with_direction, (1, 128))
    action[...] = sens[...] * (first * search[:, mine] + step * direction[:, mine])


def replicated(
    probes,
    viscosity,
    friction,
    sensitivity,
    misfit_weight,
    grad_ref,
    trace_ref,
    coarse_modes,
    coarse_inv,
    peer_slots,
    local_pairs,
    elem_agg,
):
    leaf_count = lax.axis_size("leaf")
    dim = Dims(
        viscosity.shape[0],
        viscosity.shape[1],
        2 * leaf_count,
        peer_slots.shape[2],
        coarse_modes.shape[1],
        coarse_inv.shape[0],
        lax.axis_size("probe"),
    )
    n, e, ne = dim.ndof, dim.elem, dim.total
    leaf, agg = lax.axis_index("leaf"), lax.axis_index("agg")
    order = jnp.arange(dim.half, dtype=jnp.int32)
    chips = leaf ^ order
    place = jnp.concatenate(
        [
            jnp.stack([leaf, agg, lax.axis_index("probe"), leaf]),
            chips * 2 + agg,
            chips * 2 + (1 - agg),
        ]
    ).astype(jnp.int32)
    flip = [(0, 1), (1, 0)]

    def to_partner(value):
        return lax.ppermute(value, "agg", flip)

    def peers(value):
        found = [value]
        for step in range(1, leaf_count):
            pairs = [(index, index ^ step) for index in range(leaf_count)]
            found.append(lax.ppermute(value, "leaf", pairs))
        return found

    def gather(value):
        own = peers(value)
        return own + [to_partner(one) for one in own]

    payload, quarter, sums, g3, gs, gsq3, my, m3t, trsq, inv_own = call(
        lambda *refs: source_kernel(dim, *refs),
        [
            ((n + 8, e), f32),
            ((3 * dim.share, e), f32),
            ((dim.modes, dim.group), f32),
            ((n, 3 * n), bf16),
            ((n, 6 * n), bf16),
            ((n, 3 * n), bf16),
            ((n, 3 * dim.modes), bf16),
            ((dim.modes, 3 * n), bf16),
            ((n, 1), f32),
            (coarse_inv.shape, f32),
        ],
        [place, probes, sensitivity, local_pairs, peer_slots, elem_agg.reshape(1, e)]
        + [grad_ref, trace_ref, coarse_modes, coarse_inv, viscosity, friction, misfit_weight],
        [SM] + [pltpu.HBM] * 12,
        scratch=[
            VM((n, e), f32),
            VM((n, e), f32),
            VM((2, e), jnp.int32),
            VM((dim.parts, dim.cap), jnp.int32),
            VM((1, e), jnp.int32),
            VM((n, n), f32),
            VM((n, n), f32),
            VM((n, dim.modes), f32),
            pltpu.SemaphoreType.DMA((12,)),
        ],
        flops=10**8,
    )
    (stack,) = call(stack_kernel, [((3 * dim.share * dim.half, e), f32)], peers(quarter))
    stacks = [stack]
    for step in range(1, dim.lines):
        pairs = [(index, index ^ step) for index in range(dim.lines)]
        stacks.append(lax.ppermute(stack, "probe", pairs))
    stacks += [to_partner(one) for one in stacks]
    inv_partner = to_partner(inv_own)
    sums_partner = to_partner(sums)
    (payload,) = call(
        lambda *refs: source_coarse_kernel(dim, *refs),
        [((n + 8 + dim.group, e), f32)],
        [place, payload, sums, sums_partner, inv_own, inv_partner],
        [SM, VM, VM, VM, VM, VM],
    )
    source_blocks = gather(payload)
    parts = source_blocks[: dim.half]

    field = ((n, ne), f32)
    source, lap, hot2, counts, hot_own = call(
        lambda *refs: build_kernel(dim, *refs),
        [
            field,
            ((ne, ne), bf16),
            ((dim.all_aggs, ne), bf16),
            ((1, ne), f32),
            ((dim.group, 2 * e), bf16),
        ],
        [place] + source_blocks,
        [SM] + [VM] * dim.parts,
        scratch=[VM((dim.parts, e), f32), VM((2 * dim.parts, e), f32), VM((1, ne), f32)],
    )
    work = [VM((3 * n, ne), bf16), VM((6 * n, ne), bf16)]
    image = VM((n, ne), f32)
    solved = VM((dim.all_aggs, dim.modes), f32)
    scal_shape = ((8, 128), f32)
    out_shape = ((dim.group, dim.modes), f32)
    once = 2 * ne * n * (9 * n + 2 * ne)

    visc, fric, weight, w_diag, smooth = call(
        lambda *refs: begin_kernel(dim, *refs),
        [field] * 5,
        [place, source, counts, trsq, lap, g3, gs, gsq3] + stacks,
        [SM] + [VM] * (7 + len(stacks)),
        scratch=work,
        flops=2 * once,
    )

    consts = [visc, fric, w_diag, lap, g3, gs]

    def sweep_of(first, args):
        (found,) = call(
            lambda *refs: sweep_kernel(dim, first, *refs),
            [field],
            args,
            scratch=work + ([image] if first else []),
            flops=once,
        )
        return found

    def double(parts):
        width = 2 ** (len(parts) - 1)
        if width >= leaf_count:
            return parts
        pairs = [(index, index ^ width) for index in range(leaf_count)]
        found = jnp.concatenate(parts, axis=0) if len(parts) > 1 else parts[0]
        return parts + [lax.ppermute(found, "leaf", pairs)]

    def step_of(smooth, parts):
        args = [place, smooth, visc, fric, lap, g3, gs, hot2, my, m3t, hot_own, inv_own]
        args += [inv_partner] + parts
        return call(
            lambda *refs: step_kernel(dim, *refs),
            [field, field, out_shape, table_shape],
            args,
            [SM] + [VM] * (len(args) - 1),
            scratch=work,
            flops=once,
        )

    def residual_of(source, search, image_of):
        return call(
            lambda *refs: residual_kernel(dim, *refs),
            [field, field, scal_shape],
            [source, search, image_of] + consts,
            scratch=work + [image],
            flops=once,
        )

    table_shape = ((dim.all_aggs, dim.modes), f32)
    search, image_of, out, solved_now = step_of(smooth, parts)
    parts = double([out])
    smooth, resid, scal = residual_of(source, search, image_of)
    parts = double(parts)
    smooth = sweep_of(False, [resid] + consts + [smooth])
    args = [place, smooth, resid, search, scal, solved_now, weight, visc, fric, lap, g3, gs]
    args += [hot2, my, m3t, hot_own, inv_own, inv_partner] + parts
    iterate, source_two, out = call(
        lambda *refs: middle_kernel(dim, *refs),
        [((n, e), f32), field, out_shape],
        args,
        [SM] + [VM] * (len(args) - 1),
        scratch=work + [solved, image],
        flops=once,
    )
    parts = double([out])
    smooth = sweep_of(True, [source_two] + consts)
    parts = double(parts)
    smooth = sweep_of(False, [source_two] + consts + [smooth])
    search, image_of, out, solved_now = step_of(smooth, parts)
    parts = double([out])
    smooth, resid, scal = residual_of(source_two, search, image_of)
    parts = double(parts)
    smooth = sweep_of(False, [resid] + consts + [smooth])
    args = [place, smooth, resid, search, scal, solved_now, source, sensitivity]
    args += [visc, fric, lap, g3, gs, hot2, my] + parts
    action, trace = call(
        lambda *refs: final_kernel(dim, *refs),
        [((n, e), f32), ((1, 128), f32)],
        args,
        [SM] + [VM] * (len(args) - 1),
        scratch=work + [solved, image],
        flops=once,
    )
    probe_count = lax.axis_size("probe")
    traces = [trace]
    for step in range(1, probe_count):
        pairs = [(index, (index + step) % probe_count) for index in range(probe_count)]
        if probe_count & (probe_count - 1) == 0:
            pairs = [(index, index ^ step) for index in range(probe_count)]
        traces.append(lax.ppermute(trace, "probe", pairs))
    trace_value = sum(one[0, 0] for one in traces) / probe_count
    return iterate[None], action[None], trace_value


def fits_one_core(mesh, viscosity, coarse_modes, coarse_inv, peer_slots, local_pairs):
    leaf_count, agg_count, probe_count = (mesh.shape[name] for name in ("leaf", "agg", "probe"))
    ndof, elem = viscosity.shape
    parts = leaf_count * agg_count
    cap = peer_slots.shape[2]
    aggs = coarse_inv.shape[0]
    return (
        agg_count == 2
        and leaf_count & (leaf_count - 1) == 0
        and leaf_count <= 2 ** (SWEEPS - 1)
        and elem == 128
        and coarse_modes.shape[1] == 128
        and parts * cap == elem
        and local_pairs.shape[1] == elem
        and ndof % 16 == 0
        and ndof % (8 * probe_count) == 0
        and probe_count & (probe_count - 1) == 0
        and aggs % 8 == 0
        and local_pairs.shape[1] + (parts - 1) * cap <= 256
        and parts * elem <= 1024
    )


def solution(mesh):
    in_specs = (
        P("probe", None, ("leaf", "agg")),
        P(None, ("leaf", "agg")),
        P(None, ("leaf", "agg")),
        P(None, ("leaf", "agg")),
        P(None, ("leaf", "agg")),
        P(),
        P(),
        P(),
        P(("leaf", "agg"), None, None),
        P(("leaf", "agg"), None, None),
        P(None, ("leaf", "agg")),
        P(("leaf", "agg")),
    )
    out_specs = (P("probe", None, ("leaf", "agg")), P("probe", None, ("leaf", "agg")), P())

    def on_device(*args):
        if fits_one_core(mesh, args[1], args[7], args[8], args[9], args[10]):
            return replicated(*args)
        return distributed(*args)

    return jax.shard_map(
        on_device, mesh=mesh, in_specs=in_specs, out_specs=out_specs, check_vma=False
    )
```
